128 devices in a mesh: group: 8 (over y, core), member: 16 (over z, x).
Axes of the slice: x: 4, y: 4, z: 4, core: 2. Of those that a mesh axis runs over, the one named last changes fastest.
Arguments:
- fine_blocks: float32 [2048, 5, 128, 128], P(('group', 'member')), may hold values from -6 to 6
- neighbours: int32 [2048, 5], P(('group', 'member')), may hold values from 0 to 2047, as said below
- slot_one: int32 [2048, 5], P(('group', 'member')), may hold values from 0 to 4
- pair_one: int32 [2048], P(('group', 'member')), may hold values from 0 to 1023, as said below
- prolong_one: float32 [128, 128], replicated, may hold values from -0.5 to 0.5
- slot_two: int32 [1024, 5], P(('group', 'member')), may hold values from 0 to 4
- pair_two: int32 [1024], P(('group', 'member')), may hold values from 0 to 511, as said below
- prolong_two: float32 [128, 128], replicated, may hold values from -0.5 to 0.5
- diag_inverse: float32 [2048, 128, 128], P(('group', 'member')), may hold values from -0.01953125 to 0.01953125
- right_side: float32 [2048, 128], P(('group', 'member')), may hold values from -96 to 96
- initial_guess: float32 [2048, 128], P(('group', 'member')), may hold values from -6 to 6
Outputs:
- coarse_one: float32 [1024, 5, 128, 128], P(('group', 'member'))
- coarse_two: float32 [512, 5, 128, 128], P(('group', 'member'))
- smoothed: float32 [2048, 128], P(('group', 'member'))
The draws below stay inside these ranges and needn't reach their ends.
Inputs may be any that keep to these rules, and one draw needn't show every extreme that they name: Entry 0 of a row is the row's own element; the other four are its neighbours on a periodic grid and lie in the rows of the same device or of the devices just before and just after it in group-major order, cyclically. `pair_one`: every first-level coarse row is named by exactly two fine elements. A fine element names a coarse row held by a device of its own group; the rows of one device name at most 2 rows held by any one device, and some device names exactly 2 rows of some device. `pair_two`: every second-level coarse row is named by exactly two first-level rows. A first-level row names a row held by a device with the same member index; the rows of one device name at most 2 rows held by any one device, and some device names exactly 2 rows of some device.
All inputs are finite; a program needn't handle non-finite values.
Results may differ from the reference program's by a relative error of at most 0.0001.
Values sent between devices are 32-bit elements; how exact they have to be, the bound alone decides.
A program may use at most 128 MiB of HBM per device.

```python
import jax
import jax.numpy as jnp
from jax import lax

BLOCK = 128
LINKS = 5
ROWS = 16
ELEMS = 2048
CAP_ONE = 2
CAP_TWO = 2
N_GROUP = 8
N_MEMBER = 16


def route_table(base_key, cycle_count, peer_count, row_count, capacity):
    slot_total = peer_count * capacity

    def one_cycle(cycle_key):
        sub_keys = jax.random.split(cycle_key, 6)
        forced = jax.random.randint(sub_keys[0], (), 0, peer_count)
        slot_order = jax.random.permutation(sub_keys[1], slot_total).astype(jnp.int32)
        slot_ids = jnp.arange(slot_total, dtype=jnp.int32)
        slot_score = slot_order + jnp.where(slot_ids // capacity == forced, 0, slot_total).astype(jnp.int32)
        chosen = jnp.sort(jnp.argsort(slot_score)[:row_count].astype(jnp.int32))
        shifts = chosen // capacity
        sigma_map = jax.random.permutation(sub_keys[2], peer_count).astype(jnp.int32)
        rho_map = jax.random.permutation(sub_keys[3], peer_count).astype(jnp.int32)
        positions = jax.vmap(lambda sub_key: jax.random.permutation(sub_key, row_count))(jax.random.split(sub_keys[4], peer_count)).astype(jnp.int32)
        pairing = jax.vmap(lambda sub_key: jax.random.permutation(sub_key, row_count))(jax.random.split(sub_keys[5], peer_count)).astype(jnp.int32)
        target = sigma_map[(rho_map[:, None] + shifts[positions]) % peer_count]
        coarse_local = pairing[target, positions] // 2
        return (target, coarse_local)
    return jax.vmap(one_cycle)(jax.random.split(base_key, cycle_count))


def draw_pair_one(key, part):
    target, coarse_local = route_table(jax.random.fold_in(key, 11), N_GROUP, N_MEMBER, ROWS, CAP_ONE)
    group_ids = jnp.arange(N_GROUP, dtype=jnp.int32)[:, None, None]
    owner_dev = group_ids * N_MEMBER + target
    coarse_ids = owner_dev * (ROWS // 2) + coarse_local
    return coarse_ids.reshape(-1).astype(jnp.int32)


def draw_pair_two(key, part):
    target, coarse_local = route_table(jax.random.fold_in(key, 22), N_MEMBER, N_GROUP, ROWS // 2, CAP_TWO)
    member_ids = jnp.arange(N_MEMBER, dtype=jnp.int32)[:, None, None]
    owner_dev = target * N_MEMBER + member_ids
    coarse_ids = owner_dev * (ROWS // 4) + coarse_local
    return jnp.transpose(coarse_ids, (1, 0, 2)).reshape(-1).astype(jnp.int32)


def draw_neighbours(key, part):
    device_count = ELEMS // ROWS
    sub_keys = jax.random.split(jax.random.fold_in(key, 33), device_count)
    grid_place = jax.vmap(lambda sub_key: jax.random.permutation(sub_key, ROWS))(sub_keys).astype(jnp.int32)
    inverse = jnp.argsort(grid_place, axis=1).astype(jnp.int32)
    dev_row = jnp.arange(device_count, dtype=jnp.int32)[:, None]

    def element_id(dev_ids, grid_col):
        return dev_ids * ROWS + inverse[dev_ids, grid_col]
    own_ids = dev_row * ROWS + jnp.arange(ROWS, dtype=jnp.int32)[None, :]
    west_ids = element_id(dev_row, (grid_place - 1) % ROWS)
    east_ids = element_id(dev_row, (grid_place + 1) % ROWS)
    north_ids = element_id(jnp.broadcast_to((dev_row + 1) % device_count, grid_place.shape), grid_place)
    south_ids = element_id(jnp.broadcast_to((dev_row - 1) % device_count, grid_place.shape), grid_place)
    stacked = jnp.stack([own_ids, west_ids, east_ids, north_ids, south_ids], axis=-1)
    return stacked.reshape(ELEMS, 5).astype(jnp.int32)


def place_ends(values, key, least, largest):
    shape = values.shape
    spot = [jax.random.randint(jax.random.fold_in(key, axis), (), 0, shape[axis]) for axis in range(len(shape))]
    values = values.at[tuple(spot)].set(least)
    longest = shape.index(max(shape))
    spot[longest] = (spot[longest] + 1) % shape[longest]
    return values.at[tuple(spot)].set(largest)


def block_scale(own_key, shape, cuts, low, largest):
    level = 1.0
    for position, shards_of in cuts:
        heights = jax.random.uniform(jax.random.fold_in(jax.random.fold_in(own_key, 6), position), (shards_of,), jnp.float32, low / len(cuts), largest / len(cuts))
        level = level * jnp.repeat(jnp.exp(heights), shape[position] // shards_of).reshape((-1,) + (1,) * (len(shape) - 1 - position))
    return level


def scatter_about(own_key, shape, deviation, most, shards=(), kind=jnp.bfloat16):
    result = jax.random.normal(own_key, shape, jnp.float32) * deviation
    if len(shards) > 0:
        result = block_scale(own_key, shape, shards, -0.22, 0.18) * result
    return jnp.clip(result, min=-most, max=most).astype(kind)


def setup_inputs(seed: int = 0) -> dict:
    key_list = jax.random.split(jax.random.key(seed), 12)
    return {
        "fine_blocks": scatter_about(key_list[0], (ELEMS, LINKS, BLOCK, BLOCK), 1.0, 6.0, ((0, 128),), jnp.float32),
        "neighbours": draw_neighbours(jax.random.fold_in(key_list[11], 71), 0),
        "slot_one": place_ends(jax.random.randint(key_list[2], (ELEMS, LINKS), 0, LINKS), jax.random.fold_in(key_list[2], 1), 0, LINKS - 1).astype(jnp.int32),
        "pair_one": draw_pair_one(jax.random.fold_in(key_list[11], 71), 0),
        "prolong_one": scatter_about(key_list[4], (BLOCK, BLOCK), BLOCK ** -0.5, 0.5, (), jnp.float32),
        "slot_two": place_ends(jax.random.randint(key_list[5], (ELEMS // 2, LINKS), 0, LINKS), jax.random.fold_in(key_list[5], 1), 0, LINKS - 1).astype(jnp.int32),
        "pair_two": draw_pair_two(jax.random.fold_in(key_list[11], 71), 0),
        "prolong_two": scatter_about(key_list[7], (BLOCK, BLOCK), BLOCK ** -0.5, 0.5, (), jnp.float32),
        "diag_inverse": scatter_about(key_list[8], (ELEMS, BLOCK, BLOCK), (LINKS * BLOCK * BLOCK) ** -0.5, 0.01953125, ((0, 128),), jnp.float32),
        "right_side": scatter_about(key_list[9], (ELEMS, BLOCK), 16.0, 96.0, ((0, 128),), jnp.float32),
        "initial_guess": scatter_about(key_list[10], (ELEMS, BLOCK), 1.0, 6.0, ((0, 128),), jnp.float32),
    }


damping = 0.7


def triple(blocks, prolong):
    block_shape = blocks.shape
    flat_rows = blocks.reshape(-1, block_shape[-1])
    right_part = jnp.dot(flat_rows, prolong, precision=lax.Precision.HIGHEST)
    right_part = right_part.reshape(-1, block_shape[-2], block_shape[-1])
    left_side = jnp.einsum('ua,kub->kab', prolong, right_part, precision=lax.Precision.HIGHEST)
    return left_side.reshape(block_shape)


def galerkin(blocks, slot_map, pair_map, prolong, coarse_count):
    summed = jnp.zeros((coarse_count * LINKS, BLOCK, BLOCK), jnp.float32)
    for link_index in range(LINKS):
        seg_ids = (pair_map * LINKS + slot_map[:, link_index]).astype(jnp.int32)
        summed = summed + jax.ops.segment_sum(blocks[:, link_index], seg_ids, num_segments=coarse_count * LINKS)
    return triple(summed, prolong).reshape(coarse_count, LINKS, BLOCK, BLOCK)


def reference(fine_blocks, neighbours, slot_one, pair_one, prolong_one, slot_two, pair_two, prolong_two, diag_inverse, right_side, initial_guess):
    elem_count = fine_blocks.shape[0]
    coarse_one = galerkin(fine_blocks, slot_one, pair_one, prolong_one, elem_count // 2)
    coarse_two = galerkin(coarse_one, slot_two, pair_two, prolong_two, elem_count // 4)
    nearby = initial_guess[neighbours]
    product = jnp.einsum('ekuv,ekv->eu', fine_blocks, nearby, precision=lax.Precision.HIGHEST)
    defect = right_side - product
    smoothed = initial_guess + damping * jnp.einsum('euv,ev->eu', diag_inverse, defect, precision=lax.Precision.HIGHEST)
    return coarse_one, coarse_two, smoothed
```

```python
import functools

import jax
import jax.numpy as jnp
from jax import lax
from jax.experimental import pallas as pl
from jax.experimental.pallas import tpu as pltpu
from jax.sharding import PartitionSpec as P

MESH = pl.DeviceIdType.MESH
F32 = jnp.float32
BF16 = jnp.bfloat16
I32 = jnp.int32
damping = 0.7

ROWS = 16
LINKS = 5
BLOCK = 128
MEM = 16
GRP = 8
BAND = BLOCK // MEM


def spl(a):
    hi = a.astype(BF16)
    lo = (a - hi.astype(F32)).astype(BF16)
    return hi, lo


def dot3(a, b):
    d = functools.partial(jnp.dot, preferred_element_type=F32)
    return d(a[0], b[0]) + (d(a[0], b[1]) + d(a[1], b[0]))


def kernel(
    nb_s, s1_s, p1_s, s2_s, p2_s,
    fine_h, pr1_h, pr2_h, dinv_h, rhs_h, ig_h,
    co1_h, co2_h, smo_v,
    fine, pr1, pr2, dinv, rhs, win,
    sb1, rb1, srel, rb2, sby, rby, sum2, st1, st2,
    ptab, mpair, mtwo, mpair_r, mtwo_r, tabv,
    tab_s, mtwo_s, tabx_s, tabr_s,
    lsem, msem, wsem, tsem, ssem1, rsem1, ssem2, rsem2, ssemy, rsemy, osem,
):
    g = lax.axis_index("group")
    m = lax.axis_index("member")
    y, co = g // 2, g % 2
    z, x = m // 4, m % 4
    dev = g * MEM + m
    nxt = (dev + 1) % (GRP * MEM)
    prv = (dev + GRP * MEM - 1) % (GRP * MEM)

    loads = [
        pltpu.make_async_copy(fine_h, fine, lsem.at[0]),
        pltpu.make_async_copy(ig_h, win.at[pl.ds(ROWS, ROWS)], lsem.at[1]),
        pltpu.make_async_copy(rhs_h, rhs, lsem.at[2]),
        pltpu.make_async_copy(pr1_h, pr1, lsem.at[3]),
        pltpu.make_async_copy(pr2_h, pr2, lsem.at[4]),
        pltpu.make_async_copy(dinv_h, dinv, lsem.at[5]),
    ]
    for cp in loads:
        cp.start()

    mpeers = []
    for dz, dx in sorted(
        [(dz, dx) for dz in range(4) for dx in range(4) if (dz, dx) != (0, 0)],
        key=lambda o: min(o[0], 4 - o[0]) + min(o[1], 4 - o[1]),
    ):
        mpeers.append(((z + dz) % 4) * 4 + (x + dx) % 4)
    gpeers = []
    for dy in (1, 3, 2, 0):
        for dc in range(2):
            if (dy, dc) != (0, 0):
                gpeers.append(((y + dy) % 4) * 2 + (co + dc) % 2)

    barrier = pltpu.get_barrier_semaphore()
    for t in mpeers:
        pl.semaphore_signal(barrier, inc=1, device_id=(g, t), device_id_type=MESH)
    for t in gpeers:
        pl.semaphore_signal(barrier, inc=1, device_id=(t, m), device_id_type=MESH)
    for t in (nxt, prv):
        pl.semaphore_signal(barrier, inc=1, device_id=(t // MEM, t % MEM), device_id_type=MESH)

    for e in range(ROWS):
        mpair[pl.ds(e, 1), :] = jnp.full((1, BLOCK), p1_s[e], I32)
    lane = lax.broadcasted_iota(I32, (1, BLOCK), 1)
    own2 = [p2_s[c] // (4 * MEM) for c in range(8)]
    for c in range(8):
        rank = jnp.int32(0)
        for b in range(c):
            rank = rank + jnp.where(own2[b] == own2[c], 1, 0)
        row = jnp.where(lane == 0, p2_s[c], jnp.minimum(rank, 1))
        for k in range(LINKS):
            row = jnp.where(lane == 1 + k, s2_s[c, k], row)
        mtwo[pl.ds(c, 1), :] = row
    for gp in range(GRP):
        a0 = jnp.int32(0)
        a1 = jnp.int32(0)
        for c in reversed(range(8)):
            hit = own2[c] == gp
            a1 = jnp.where(hit, a0, a1)
            a0 = jnp.where(hit, c, a0)
        tabx_s[2 * gp] = a0
        tabx_s[2 * gp + 1] = a1

    pl.semaphore_wait(barrier, MEM - 1 + GRP - 1 + 2)

    def remote(src, dst, ss, rs, dev_id):
        pltpu.make_async_remote_copy(
            src_ref=src, dst_ref=dst, send_sem=ss, recv_sem=rs, device_id=dev_id, device_id_type=MESH
        ).start()

    def local(src, dst, s):
        pltpu.make_async_copy(src, dst, s).start()

    for t in mpeers:
        remote(mpair, mpair_r.at[m], msem.at[0], msem.at[1], (g, t))
    local(mpair, mpair_r.at[m], msem.at[1])
    for t in gpeers:
        remote(mtwo, mtwo_r.at[g], msem.at[2], msem.at[3], (t, m))
    local(mtwo, mtwo_r.at[g], msem.at[3])

    def slotted(s):
        @pl.loop(0, ROWS)
        def _(e):
            acc = jnp.where(s1_s[e, 0] == s, 1.0, 0.0) * fine[e, 0]
            for k in range(1, LINKS):
                acc = acc + jnp.where(s1_s[e, k] == s, 1.0, 0.0) * fine[e, k]
            sb1[s, :, e] = acc.reshape(MEM, BAND, BLOCK)

    def send1(s):
        for t in mpeers:
            remote(
                sb1.at[s, t], rb1[s].at[pl.ds(pl.multiple_of(m * ROWS, ROWS), ROWS)],
                ssem1.at[s], rsem1.at[s], (g, t),
            )
        local(sb1.at[s, m], rb1[s].at[pl.ds(pl.multiple_of(m * ROWS, ROWS), ROWS)], rsem1.at[s])

    def relay(s):
        @pl.loop(0, MEM * 8 // 8)
        def _(i):
            for b in range(8):
                c = i * 8 + b
                srel[s, c] = rb1[s][tab_s[0, 0, c]] + rb1[s][tab_s[1, 0, c]]

    def send2(s):
        for t in mpeers:
            remote(
                srel.at[s, pl.ds(pl.multiple_of(t * 8, 8), 8)], rb2[s].at[m],
                ssem2.at[s], rsem2.at[s], (g, t),
            )
        local(srel.at[s, pl.ds(pl.multiple_of(m * 8, 8), 8)], rb2[s].at[m], rsem2.at[s])

    def sendy(s):
        for gp in range(GRP):
            for j in range(2):
                sby[s, gp, j] = rb2[s][:, tabx_s[2 * gp + j]]
        for t in gpeers:
            remote(sby.at[s, t], rby[s].at[g], ssemy.at[s], rsemy.at[s], (t, m))
        local(sby.at[s, g], rby[s].at[g], rsemy.at[s])

    def addy(s):
        @pl.loop(0, 4)
        def _(q):
            rs, ws = [], []
            for i in range(2):
                code = tabr_s[q * 2 + i]
                src = code // 8
                c = code % 8
                rs.append(rby[s][src, jnp.clip(mtwo_s[src, c, 6], 0, 1)])
                ws.append(mtwo_s[src, c, 1 + s])
            for t in range(LINKS):
                add = jnp.where(ws[0] == t, 1.0, 0.0) * rs[0] + jnp.where(ws[1] == t, 1.0, 0.0) * rs[1]
                if s == 0:
                    sum2[q, t] = add
                else:
                    sum2[q, t] = sum2[q, t] + add

    def wait1(s):
        pltpu.make_async_copy(rb1[s], rb1[s], rsem1.at[s]).wait()

    def wait2(s):
        pltpu.make_async_copy(rb2[s], rb2[s], rsem2.at[s]).wait()

    def waity(s):
        pltpu.make_async_copy(rby[s], rby[s], rsemy.at[s]).wait()

    loads[0].wait()
    slotted(0)
    send1(0)
    slotted(1)
    send1(1)
    loads[1].wait()
    remote(
        win.at[pl.ds(ROWS, ROWS)], win.at[pl.ds(0, ROWS)], wsem.at[0], wsem.at[2],
        (nxt // MEM, nxt % MEM),
    )
    remote(
        win.at[pl.ds(ROWS, ROWS)], win.at[pl.ds(2 * ROWS, ROWS)], wsem.at[1], wsem.at[3],
        (prv // MEM, prv % MEM),
    )
    for s in range(2, LINKS):
        slotted(s)

    pltpu.make_async_copy(mpair_r, mpair_r, msem.at[1]).wait()
    cid = lax.broadcasted_iota(I32, (8, BLOCK), 1) + g * (MEM * 8)
    sub = lax.broadcasted_iota(I32, (8, BLOCK), 0)
    lo = jnp.full((8, BLOCK), 1 << 20, I32)
    hi = jnp.full((8, BLOCK), -1, I32)
    for src in range(MEM):
        for h in range(2):
            hit = mpair_r[src, pl.ds(8 * h, 8), :] == cid
            eid = sub + (src * ROWS + 8 * h)
            lo = jnp.minimum(lo, jnp.where(hit, eid, 1 << 20))
            hi = jnp.maximum(hi, jnp.where(hit, eid, -1))
    for sh in (4, 2, 1):
        lo = jnp.minimum(lo, pltpu.roll(lo, sh, 0))
        hi = jnp.maximum(hi, pltpu.roll(hi, sh, 0))
    tabv[0] = jnp.clip(lo, 0, MEM * ROWS - 1)
    tabv[1] = jnp.clip(hi, 0, MEM * ROWS - 1)
    pltpu.make_async_copy(mtwo_r, mtwo_r, msem.at[3]).wait()
    cp_t = pltpu.make_async_copy(tabv, tab_s, tsem.at[0])
    cp_t.start()
    cp_m = pltpu.make_async_copy(mtwo_r, mtwo_s, tsem.at[1])
    cp_m.start()
    cp_t.wait()
    cp_m.wait()
    qbase = dev * 4

    def scan(i, carry):
        v = mtwo_s[i // 8, i % 8, 0]
        out = []
        for q in range(4):
            p0, p1 = carry[2 * q], carry[2 * q + 1]
            hit = v == qbase + q
            out.append(jnp.where(hit, i, p0))
            out.append(jnp.where(hit, p0, p1))
        return tuple(out)

    found = lax.fori_loop(0, 64, scan, tuple(jnp.int32(0) for _ in range(8)))
    for i in range(8):
        tabr_s[i] = found[i]

    for cp in loads[2:]:
        cp.wait()
    pltpu.make_async_copy(win.at[pl.ds(0, ROWS)], win.at[pl.ds(0, ROWS)], wsem.at[2]).wait()
    pltpu.make_async_copy(win.at[pl.ds(0, ROWS)], win.at[pl.ds(2 * ROWS, ROWS)], wsem.at[3]).wait()
    lanes = lax.broadcasted_iota(I32, (BLOCK, BLOCK), 1)
    total = GRP * MEM * ROWS

    def prod(e, cols):
        acc = jnp.zeros((BLOCK, BLOCK), F32)
        for k in range(LINKS):
            at = nb_s[e, k] - dev * ROWS + ROWS
            at = jnp.where(at < 0, at + total, jnp.where(at >= total, at - total, at))
            at = jnp.clip(at, 0, 3 * ROWS - 1)
            acc = acc + fine[e, k] * win[pl.ds(at, 1), :]
        return jnp.where(lanes == e, jnp.sum(acc, axis=1, keepdims=True), cols)

    cols = lax.fori_loop(0, ROWS, prod, jnp.zeros((BLOCK, BLOCK), F32))
    rhs[...] = rhs[...] - cols.T[:ROWS]

    def smooth(e, cols):
        acc = dinv[e] * rhs[pl.ds(e, 1), :]
        return jnp.where(lanes == e, jnp.sum(acc, axis=1, keepdims=True), cols)

    cols = lax.fori_loop(0, ROWS, smooth, jnp.zeros((BLOCK, BLOCK), F32))
    smo_v[...] = win[pl.ds(ROWS, ROWS), :] + damping * cols.T[:ROWS]

    p1 = pr1[...]
    p1r, p1l = spl(p1), spl(p1.T)
    qm = jnp.dot(p1, pr2[...], preferred_element_type=F32, precision=lax.Precision.HIGHEST)
    for i, a in enumerate((*p1r, *p1l, *spl(qm), *spl(qm.T))):
        ptab[i] = a

    def triple(blk, o):
        right = dot3(spl(blk), (ptab[o], ptab[o + 1]))
        return dot3((ptab[o + 2], ptab[o + 3]), spl(right))

    def coarse(s):
        @pl.loop(0, 2)
        def _(i):
            for b in range(4):
                c = i * 4 + b
                st1[s, c] = triple(rb2[s][:, c].reshape(BLOCK, BLOCK), 0)
        pltpu.make_async_copy(st1.at[s], co1_h.at[:, s], osem.at[s]).start()

    for s in range(LINKS):
        wait1(s)
        relay(s)
        send2(s)
        if s + 2 < LINKS:
            send1(s + 2)
        if s >= 1:
            wait2(s - 1)
            sendy(s - 1)
            coarse(s - 1)
        if s >= 2:
            waity(s - 2)
            addy(s - 2)
    last = LINKS - 1
    wait2(last)
    sendy(last)
    waity(last - 1)
    addy(last - 1)
    coarse(last)
    waity(last)
    addy(last)

    @pl.loop(0, 5)
    def _(i):
        for b in range(4):
            j = i * 4 + b
            st2[j] = triple(sum2[j // 5, j % 5].reshape(BLOCK, BLOCK), 4)

    cp2 = pltpu.make_async_copy(st2, co2_h, osem.at[LINKS])
    cp2.start()
    for s in range(LINKS):
        pltpu.make_async_copy(sb1.at[s, pl.ds(0, MEM - 1)], sb1.at[s, pl.ds(0, MEM - 1)], ssem1.at[s]).wait()
        pltpu.make_async_copy(rb2[s].at[pl.ds(0, MEM - 1)], rb2[s].at[pl.ds(0, MEM - 1)], ssem2.at[s]).wait()
        pltpu.make_async_copy(sby.at[s, pl.ds(0, GRP - 1)], sby.at[s, pl.ds(0, GRP - 1)], ssemy.at[s]).wait()
        pltpu.make_async_copy(st1.at[s], co1_h.at[:, s], osem.at[s]).wait()
    pltpu.make_async_copy(mpair_r.at[pl.ds(0, MEM - 1)], mpair_r.at[pl.ds(0, MEM - 1)], msem.at[0]).wait()
    pltpu.make_async_copy(mtwo_r.at[pl.ds(0, GRP - 1)], mtwo_r.at[pl.ds(0, GRP - 1)], msem.at[2]).wait()
    for i in range(2):
        pltpu.make_async_copy(win.at[pl.ds(0, ROWS)], win.at[pl.ds(0, ROWS)], wsem.at[i]).wait()
    cp2.wait()


def local(
    fine_blocks, neighbours, slot_one, pair_one, prolong_one, slot_two, pair_two, prolong_two,
    diag_inverse, right_side, initial_guess,
):
    smem = pl.BlockSpec(memory_space=pltpu.SMEM)
    hbm = pl.BlockSpec(memory_space=pl.ANY)
    vmem = pl.BlockSpec(memory_space=pltpu.VMEM)
    V, S, D = pltpu.VMEM, pltpu.SMEM, pltpu.SemaphoreType.DMA
    co1, co2, smo = pl.pallas_call(
        kernel,
        name="setup",
        out_shape=(
            jax.ShapeDtypeStruct((8, LINKS, BLOCK, BLOCK), F32),
            jax.ShapeDtypeStruct((4 * LINKS, BLOCK, BLOCK), F32),
            jax.ShapeDtypeStruct((ROWS, BLOCK), F32),
        ),
        in_specs=[smem] * 5 + [hbm] * 6,
        out_specs=(hbm, hbm, vmem),
        scratch_shapes=[
            V((ROWS, LINKS, BLOCK, BLOCK), F32),
            V((BLOCK, BLOCK), F32),
            V((BLOCK, BLOCK), F32),
            V((ROWS, BLOCK, BLOCK), F32),
            V((ROWS, BLOCK), F32),
            V((3 * ROWS, BLOCK), F32),
            V((LINKS, MEM, ROWS, BAND, BLOCK), F32),
            [V((MEM * ROWS, BAND, BLOCK), F32)] * LINKS,
            V((LINKS, MEM * 8, BAND, BLOCK), F32),
            [V((MEM, 8, BAND, BLOCK), F32)] * LINKS,
            V((LINKS, GRP, 2, MEM, BAND, BLOCK), F32),
            [V((GRP, 2, MEM, BAND, BLOCK), F32)] * LINKS,
            V((4, LINKS, MEM, BAND, BLOCK), F32),
            V((LINKS, 8, BLOCK, BLOCK), F32),
            V((4 * LINKS, BLOCK, BLOCK), F32),
            V((8, BLOCK, BLOCK), BF16),
            V((ROWS, BLOCK), I32),
            V((8, BLOCK), I32),
            V((MEM, ROWS, BLOCK), I32),
            V((GRP, 8, BLOCK), I32),
            V((2, 8, BLOCK), I32),
            S((2, 8, BLOCK), I32),
            S((GRP, 8, BLOCK), I32),
            S((2 * GRP,), I32),
            S((8,), I32),
            D((6,)), D((4,)), D((4,)), D((2,)),
            D((LINKS,)), D((LINKS,)), D((LINKS,)), D((LINKS,)), D((LINKS,)), D((LINKS,)),
            D((LINKS + 1,)),
        ],
        compiler_params=pltpu.CompilerParams(
            collective_id=0, has_side_effects=True, vmem_limit_bytes=60 * 1024 * 1024
        ),
    )(
        neighbours, slot_one, pair_one, slot_two, pair_two,
        fine_blocks, prolong_one, prolong_two, diag_inverse, right_side, initial_guess,
    )
    return co1, co2.reshape(4, LINKS, BLOCK, BLOCK), smo


def solution(mesh):
    both = ("group", "member")
    return jax.shard_map(
        local,
        mesh=mesh,
        in_specs=(
            P(both, None, None, None), P(both, None), P(both, None), P(both), P(), P(both, None), P(both), P(),
            P(both, None, None), P(both, None), P(both, None),
        ),
        out_specs=(P(both, None, None, None), P(both, None, None, None), P(both, None)),
        check_vma=False,
    )
```

```python
import functools

import jax
import jax.numpy as jnp
from jax import lax
from jax.experimental import pallas as pl
from jax.experimental.pallas import tpu as pltpu
from jax.sharding import PartitionSpec as P

MESH = pl.DeviceIdType.MESH
F32 = jnp.float32
BF16 = jnp.bfloat16
I32 = jnp.int32
damping = 0.7

ROWS = 16
LINKS = 5
BLOCK = 128
MEM = 16
GRP = 8
BAND = BLOCK // MEM
LIMIT = 60 * 1024 * 1024


def spl(a):
    hi = a.astype(BF16)
    lo = (a - hi.astype(F32)).astype(BF16)
    return hi, lo


def dot3(a, b):
    d = functools.partial(jnp.dot, preferred_element_type=F32)
    return d(a[0], b[0]) + (d(a[0], b[1]) + d(a[1], b[0]))


def triple(blk, tab):
    right = dot3(spl(blk), (tab[0], tab[1]))
    return dot3((tab[2], tab[3]), spl(right))


def finish(co1, sum2, qtab, smo, co1_o, co2_o, smo_o, st2, sem):
    out = [
        pltpu.make_async_copy(co1, co1_o, sem.at[0]),
        pltpu.make_async_copy(smo, smo_o, sem.at[1]),
    ]
    for cp in out:
        cp.start()
    for i in range(5):
        for b in range(4):
            j = i * 4 + b
            st2[j] = triple(sum2[j].reshape(BLOCK, BLOCK), qtab)
        out.append(pltpu.make_async_copy(st2.at[pl.ds(4 * i, 4)], co2_o.at[pl.ds(4 * i, 4)], sem.at[2 + i]))
        out[-1].start()
    for cp in out:
        cp.wait()


def kernel(
    nb_s, s1_s, p1_s, s2_s, p2_s,
    fine_h, pr1_h, pr2_h, dinv_h, rhs_h, ig_h,
    co1, sum2, qtab, smo_v,
    fine, pr1, pr2, dinv, rhs, win,
    sb1, rb1, srel, rb2, sby, rby, blk, cols_v,
    ptab, mpair, mtwo, mpair_r, mtwo_r, tabv,
    tab_s, mtwo_s, tabx_s, tabr_s,
    lsem, msem, wsem, tsem, ssem1, rsem1, ssem2, rsem2, ssemy, rsemy,
):
    g = lax.axis_index("group")
    m = lax.axis_index("member")
    y, co = g // 2, g % 2
    z, x = m // 4, m % 4
    dev = g * MEM + m
    nxt = (dev + 1) % (GRP * MEM)
    prv = (dev + GRP * MEM - 1) % (GRP * MEM)

    loads = [
        pltpu.make_async_copy(fine_h, fine, lsem.at[0]),
        pltpu.make_async_copy(ig_h, win.at[pl.ds(ROWS, ROWS)], lsem.at[1]),
        pltpu.make_async_copy(rhs_h, rhs, lsem.at[2]),
        pltpu.make_async_copy(pr1_h, pr1, lsem.at[3]),
        pltpu.make_async_copy(pr2_h, pr2, lsem.at[4]),
        pltpu.make_async_copy(dinv_h, dinv, lsem.at[5]),
    ]
    for cp in loads:
        cp.start()

    order = sorted(
        [(dz, dx) for dz in range(4) for dx in range(4)],
        key=lambda o: min(o[0], 4 - o[0]) + min(o[1], 4 - o[1]),
    )
    ahead = [((z + dz) % 4) * 4 + (x + dx) % 4 for dz, dx in order]
    behind = [((z + 4 - dz) % 4) * 4 + (x + 4 - dx) % 4 for dz, dx in order]
    mpeers = ahead[1:]
    gpeers = []
    for dy in (1, 3, 2, 0):
        for dc in range(2):
            if (dy, dc) != (0, 0):
                gpeers.append(((y + dy) % 4) * 2 + (co + dc) % 2)

    barrier = pltpu.get_barrier_semaphore()
    for t in mpeers:
        pl.semaphore_signal(barrier, inc=1, device_id=(g, t), device_id_type=MESH)
    for t in gpeers:
        pl.semaphore_signal(barrier, inc=1, device_id=(t, m), device_id_type=MESH)
    for t in (nxt, prv):
        pl.semaphore_signal(barrier, inc=1, device_id=(t // MEM, t % MEM), device_id_type=MESH)

    for e in range(ROWS):
        mpair[pl.ds(e, 1), :] = jnp.full((1, BLOCK), p1_s[e], I32)
    lane = lax.broadcasted_iota(I32, (1, BLOCK), 1)
    own2 = [p2_s[c] // (4 * MEM) for c in range(8)]
    for c in range(8):
        rank = jnp.int32(0)
        for b in range(c):
            rank = rank + jnp.where(own2[b] == own2[c], 1, 0)
        row = jnp.where(lane == 0, p2_s[c], jnp.minimum(rank, 1))
        for k in range(LINKS):
            row = jnp.where(lane == 1 + k, s2_s[c, k], row)
        mtwo[pl.ds(c, 1), :] = row
    for gp in range(GRP):
        a0 = jnp.int32(0)
        a1 = jnp.int32(0)
        for c in reversed(range(8)):
            hit = own2[c] == gp
            a1 = jnp.where(hit, a0, a1)
            a0 = jnp.where(hit, c, a0)
        tabx_s[2 * gp] = a0
        tabx_s[2 * gp + 1] = a1

    pl.semaphore_wait(barrier, MEM - 1 + GRP - 1 + 2)

    def remote(src, dst, ss, rs, dev_id):
        pltpu.make_async_remote_copy(
            src_ref=src, dst_ref=dst, send_sem=ss, recv_sem=rs, device_id=dev_id, device_id_type=MESH
        ).start()

    def local(src, dst, s):
        pltpu.make_async_copy(src, dst, s).start()

    for t in mpeers:
        remote(mpair, mpair_r.at[m], msem.at[0], msem.at[1], (g, t))
    local(mpair, mpair_r.at[m], msem.at[1])
    for t in gpeers:
        remote(mtwo, mtwo_r.at[g], msem.at[2], msem.at[3], (t, m))
    local(mtwo, mtwo_r.at[g], msem.at[3])

    def slotted(s):
        @pl.loop(0, ROWS)
        def _(e):
            acc = jnp.where(s1_s[0, e] == s, 1.0, 0.0) * fine[e, 0]
            for k in range(1, LINKS):
                acc = acc + jnp.where(s1_s[k, e] == s, 1.0, 0.0) * fine[e, k]
            sb1[s, :, e] = acc.reshape(MEM, BAND, BLOCK)

    def send1(s):
        for t in mpeers:
            remote(
                sb1.at[s, t], rb1[s].at[pl.ds(pl.multiple_of(m * ROWS, ROWS), ROWS)],
                ssem1.at[s], rsem1.at[s], (g, t),
            )
        local(sb1.at[s, m], rb1[s].at[pl.ds(pl.multiple_of(m * ROWS, ROWS), ROWS)], rsem1.at[s])

    def relay(s):
        @pl.loop(0, MEM * 8 // 8)
        def _(i):
            for b in range(8):
                c = i * 8 + b
                srel[s, c] = rb1[s][tab_s[0, 0, c]] + rb1[s][tab_s[1, 0, c]]

    def send2(s):
        local(srel.at[s, pl.ds(pl.multiple_of(m * 8, 8), 8)], rb2[2 * s].at[0], rsem2.at[2 * s])
        for i in range(1, MEM):
            h, t = 2 * s + i // 8, ahead[i]
            remote(
                srel.at[s, pl.ds(pl.multiple_of(t * 8, 8), 8)], rb2[h].at[i % 8],
                ssem2.at[s], rsem2.at[h], (g, t),
            )

    def sendy(s, h):
        p = 2 * s + h
        pltpu.make_async_copy(rb2[p], rb2[p], rsem2.at[p]).wait()
        for gp in range(GRP):
            for j in range(2):
                sby[p, gp, j] = rb2[p][:, tabx_s[2 * gp + j]]
        for t in gpeers:
            remote(sby.at[p, t], rby[p].at[g], ssemy.at[s], rsemy.at[p], (t, m))
        local(sby.at[p, g], rby[p].at[g], rsemy.at[p])

    def addy(s, h):
        p = 2 * s + h
        pltpu.make_async_copy(rby[p], rby[p], rsemy.at[p]).wait()

        @pl.loop(0, 4)
        def _(q):
            rs, ws = [], []
            for i in range(2):
                code = tabr_s[q * 2 + i]
                src = code // 8
                c = code % 8
                rs.append(rby[p][src, jnp.clip(mtwo_s[src, c, 6], 0, 1)])
                ws.append(mtwo_s[src, c, 1 + s])
            for t in range(LINKS):
                add = jnp.where(ws[0] == t, 1.0, 0.0) * rs[0] + jnp.where(ws[1] == t, 1.0, 0.0) * rs[1]
                for i in range(8):
                    b = behind[8 * h + i]
                    if s == 0:
                        sum2[q * LINKS + t, b] = add[i]
                    else:
                        sum2[q * LINKS + t, b] = sum2[q * LINKS + t, b] + add[i]

    def wait1(s):
        pltpu.make_async_copy(rb1[s], rb1[s], rsem1.at[s]).wait()

    loads[0].wait()
    slotted(0)
    send1(0)
    slotted(1)
    send1(1)
    loads[1].wait()
    remote(
        win.at[pl.ds(ROWS, ROWS)], win.at[pl.ds(0, ROWS)], wsem.at[0], wsem.at[2],
        (nxt // MEM, nxt % MEM),
    )
    remote(
        win.at[pl.ds(ROWS, ROWS)], win.at[pl.ds(2 * ROWS, ROWS)], wsem.at[1], wsem.at[3],
        (prv // MEM, prv % MEM),
    )
    slotted(2)

    pltpu.make_async_copy(mpair_r, mpair_r, msem.at[1]).wait()
    cid = lax.broadcasted_iota(I32, (8, BLOCK), 1) + g * (MEM * 8)
    sub = lax.broadcasted_iota(I32, (8, BLOCK), 0)
    lo = jnp.full((8, BLOCK), 1 << 20, I32)
    hi = jnp.full((8, BLOCK), -1, I32)
    for src in range(MEM):
        for h in range(2):
            hit = mpair_r[src, pl.ds(8 * h, 8), :] == cid
            eid = sub + (src * ROWS + 8 * h)
            lo = jnp.minimum(lo, jnp.where(hit, eid, 1 << 20))
            hi = jnp.maximum(hi, jnp.where(hit, eid, -1))
    for sh in (4, 2, 1):
        lo = jnp.minimum(lo, pltpu.roll(lo, sh, 0))
        hi = jnp.maximum(hi, pltpu.roll(hi, sh, 0))
    tabv[0] = jnp.clip(lo, 0, MEM * ROWS - 1)
    tabv[1] = jnp.clip(hi, 0, MEM * ROWS - 1)
    pltpu.make_async_copy(mtwo_r, mtwo_r, msem.at[3]).wait()
    cp_t = pltpu.make_async_copy(tabv, tab_s, tsem.at[0])
    cp_t.start()
    cp_m = pltpu.make_async_copy(mtwo_r, mtwo_s, tsem.at[1])
    cp_m.start()
    cp_t.wait()
    cp_m.wait()
    qbase = dev * 4

    def scan(i, carry):
        v = mtwo_s[i // 8, i % 8, 0]
        out = []
        for q in range(4):
            p0, p1 = carry[2 * q], carry[2 * q + 1]
            hit = v == qbase + q
            out.append(jnp.where(hit, i, p0))
            out.append(jnp.where(hit, p0, p1))
        return tuple(out)

    found = lax.fori_loop(0, 64, scan, tuple(jnp.int32(0) for _ in range(8)))
    for i in range(8):
        tabr_s[i] = found[i]

    lanes = lax.broadcasted_iota(I32, (BLOCK, BLOCK), 1)
    total = GRP * MEM * ROWS

    def prod(e, cols):
        acc = jnp.zeros((BLOCK, BLOCK), F32)
        for k in range(LINKS):
            at = nb_s[k, e] - dev * ROWS + ROWS
            at = jnp.where(at < 0, at + total, jnp.where(at >= total, at - total, at))
            at = jnp.clip(at, 0, 3 * ROWS - 1)
            acc = acc + fine[e, k] * win[pl.ds(at, 1), :]
        return jnp.where(lanes == e, jnp.sum(acc, axis=1, keepdims=True), cols)

    def smooth(e, cols):
        acc = dinv[e] * rhs[pl.ds(e, 1), :]
        return jnp.where(lanes == e, jnp.sum(acc, axis=1, keepdims=True), cols)

    def sweep(part):
        if part == 0:
            for cp in loads[2:]:
                cp.wait()
            pltpu.make_async_copy(win.at[pl.ds(0, ROWS)], win.at[pl.ds(0, ROWS)], wsem.at[2]).wait()
            pltpu.make_async_copy(win.at[pl.ds(0, ROWS)], win.at[pl.ds(2 * ROWS, ROWS)], wsem.at[3]).wait()
            cols_v[...] = lax.fori_loop(0, 8, prod, jnp.zeros((BLOCK, BLOCK), F32))
        elif part == 1:
            cols = lax.fori_loop(8, ROWS, prod, cols_v[...])
            rhs[...] = rhs[...] - cols.T[:ROWS]
        else:
            cols = lax.fori_loop(0, ROWS, smooth, jnp.zeros((BLOCK, BLOCK), F32))
            smo_v[...] = win[pl.ds(ROWS, ROWS), :] + damping * cols.T[:ROWS]

    def products():
        p1 = pr1[...]
        qm = jnp.dot(p1, pr2[...], preferred_element_type=F32, precision=lax.Precision.HIGHEST)
        for i, a in enumerate((*spl(p1), *spl(p1.T))):
            ptab[i] = a
        for i, a in enumerate((*spl(qm), *spl(qm.T))):
            qtab[i] = a

    def coarse(s):
        for h in range(2):
            for i in range(8):
                blk[:, behind[8 * h + i]] = rb2[2 * s + h][i]

        @pl.loop(0, 2)
        def _(i):
            for b in range(4):
                c = i * 4 + b
                co1[c, s] = triple(blk[c].reshape(BLOCK, BLOCK), ptab)

    def hop(s, then):
        wait1(s)
        relay(s)
        send2(s)
        if then is not None:
            send1(then)

    def up(s):
        sendy(s, 0)
        sendy(s, 1)
        coarse(s)

    def done(s):
        addy(s, 0)
        addy(s, 1)

    hop(0, 2)
    sweep(0)
    slotted(3)
    products()
    hop(1, 3)
    slotted(4)
    up(0)
    sweep(1)
    hop(2, None)
    up(1)
    done(0)
    sweep(2)
    hop(3, 4)
    up(2)
    done(1)
    up(3)
    done(2)
    hop(4, None)
    up(4)
    done(3)
    done(4)
    for s in range(LINKS):
        pltpu.make_async_copy(sb1.at[s, pl.ds(0, MEM - 1)], sb1.at[s, pl.ds(0, MEM - 1)], ssem1.at[s]).wait()
        pltpu.make_async_copy(srel.at[s, pl.ds(0, 120)], srel.at[s, pl.ds(0, 120)], ssem2.at[s]).wait()
        pltpu.make_async_copy(
            sby.at[pl.ds(2 * s, 2), pl.ds(0, GRP - 1)], sby.at[pl.ds(2 * s, 2), pl.ds(0, GRP - 1)], ssemy.at[s]
        ).wait()
    pltpu.make_async_copy(mpair_r.at[pl.ds(0, MEM - 1)], mpair_r.at[pl.ds(0, MEM - 1)], msem.at[0]).wait()
    pltpu.make_async_copy(mtwo_r.at[pl.ds(0, GRP - 1)], mtwo_r.at[pl.ds(0, GRP - 1)], msem.at[2]).wait()
    for i in range(2):
        pltpu.make_async_copy(win.at[pl.ds(0, ROWS)], win.at[pl.ds(0, ROWS)], wsem.at[i]).wait()


def local(
    fine_blocks, neighbours, slot_one, pair_one, prolong_one, slot_two, pair_two, prolong_two,
    diag_inverse, right_side, initial_guess,
):
    smem = pl.BlockSpec(memory_space=pltpu.SMEM)
    hbm = pl.BlockSpec(memory_space=pltpu.HBM)
    vmem = pl.BlockSpec(memory_space=pltpu.VMEM)
    V, S, D = pltpu.VMEM, pltpu.SMEM, pltpu.SemaphoreType.DMA
    mid = pl.pallas_call(
        kernel,
        name="setup",
        out_shape=(
            V((8, LINKS, BLOCK, BLOCK), F32),
            V((4 * LINKS, MEM, BAND, BLOCK), F32),
            V((4, BLOCK, BLOCK), BF16),
            V((ROWS, BLOCK), F32),
        ),
        in_specs=[smem] * 5 + [hbm] * 6,
        out_specs=(vmem,) * 4,
        scratch_shapes=[
            V((ROWS, LINKS, BLOCK, BLOCK), F32),
            V((BLOCK, BLOCK), F32),
            V((BLOCK, BLOCK), F32),
            V((ROWS, BLOCK, BLOCK), F32),
            V((ROWS, BLOCK), F32),
            V((3 * ROWS, BLOCK), F32),
            V((LINKS, MEM, ROWS, BAND, BLOCK), F32),
            [V((MEM * ROWS, BAND, BLOCK), F32)] * LINKS,
            V((LINKS, MEM * 8, BAND, BLOCK), F32),
            [V((8, 8, BAND, BLOCK), F32)] * (2 * LINKS),
            V((2 * LINKS, GRP, 2, 8, BAND, BLOCK), F32),
            [V((GRP, 2, 8, BAND, BLOCK), F32)] * (2 * LINKS),
            V((8, MEM, BAND, BLOCK), F32),
            V((BLOCK, BLOCK), F32),
            V((4, BLOCK, BLOCK), BF16),
            V((ROWS, BLOCK), I32),
            V((8, BLOCK), I32),
            V((MEM, ROWS, BLOCK), I32),
            V((GRP, 8, BLOCK), I32),
            V((2, 8, BLOCK), I32),
            S((2, 8, BLOCK), I32),
            S((GRP, 8, BLOCK), I32),
            S((2 * GRP,), I32),
            S((8,), I32),
            D((6,)), D((4,)), D((4,)), D((2,)),
            D((LINKS,)), D((LINKS,)), D((LINKS,)), D((2 * LINKS,)), D((LINKS,)), D((2 * LINKS,)),
        ],
        compiler_params=pltpu.CompilerParams(
            collective_id=0, has_side_effects=True, vmem_limit_bytes=LIMIT
        ),
    )(
        neighbours.T, slot_one.T, pair_one, slot_two, pair_two,
        fine_blocks, prolong_one, prolong_two, diag_inverse, right_side, initial_guess,
    )
    co1, co2, smo = pl.pallas_call(
        finish,
        name="finish",
        out_shape=(
            jax.ShapeDtypeStruct((8, LINKS, BLOCK, BLOCK), F32),
            jax.ShapeDtypeStruct((4 * LINKS, BLOCK, BLOCK), F32),
            jax.ShapeDtypeStruct((ROWS, BLOCK), F32),
        ),
        in_specs=[vmem] * 4,
        out_specs=(hbm,) * 3,
        scratch_shapes=[V((4 * LINKS, BLOCK, BLOCK), F32), D((7,))],
        compiler_params=pltpu.CompilerParams(vmem_limit_bytes=16 * 1024 * 1024),
    )(*mid)
    return co1, co2.reshape(4, LINKS, BLOCK, BLOCK), smo


def solution(mesh):
    both = ("group", "member")
    return jax.shard_map(
        local,
        mesh=mesh,
        in_specs=(
            P(both, None, None, None), P(both, None), P(both, None), P(both), P(), P(both, None), P(both), P(),
            P(both, None, None), P(both, None), P(both, None),
        ),
        out_specs=(P(both, None, None, None), P(both, None, None, None), P(both, None)),
        check_vma=False,
    )
```

```python
import functools

import jax
import jax.numpy as jnp
from jax import lax
from jax.experimental import pallas as pl
from jax.experimental.pallas import tpu as pltpu
from jax.sharding import PartitionSpec as P

MESH = pl.DeviceIdType.MESH
F32 = jnp.float32
BF16 = jnp.bfloat16
I32 = jnp.int32
damping = 0.7

ROWS = 16
LINKS = 5
BLOCK = 128
MEM = 16
GRP = 8
BAND = BLOCK // MEM
LIMIT = 60 * 1024 * 1024


def spl(a):
    hi = a.astype(BF16)
    lo = (a - hi.astype(F32)).astype(BF16)
    return hi, lo


def dot3(a, b):
    d = functools.partial(jnp.dot, preferred_element_type=F32)
    return d(a[0], b[0]) + (d(a[0], b[1]) + d(a[1], b[0]))


def triple(blk, tab):
    right = dot3(spl(blk), (tab[0], tab[1]))
    return dot3((tab[2], tab[3]), spl(right))


def finish(co1, sum2, qtab, smo, co1_o, co2_o, smo_o, st2, sem):
    out = [
        pltpu.make_async_copy(co1, co1_o, sem.at[0]),
        pltpu.make_async_copy(smo, smo_o, sem.at[1]),
    ]
    for cp in out:
        cp.start()
    for i in range(5):
        for b in range(4):
            j = i * 4 + b
            st2[j] = triple(sum2[j].reshape(BLOCK, BLOCK), qtab)
        out.append(pltpu.make_async_copy(st2.at[pl.ds(4 * i, 4)], co2_o.at[pl.ds(4 * i, 4)], sem.at[2 + i]))
        out[-1].start()
    for cp in out:
        cp.wait()


def kernel(
    nb_s, s1_s, p1_s, s2_s, p2_s,
    fine_h, pr1_h, pr2_h, dinv_h, rhs_h, ig_h,
    co1, sum2, qtab, smo_v,
    fine, pr1, pr2, dinv, rhs, win,
    sb1, rb1, srel, rb2, sby, rby, blk, cols_v,
    ptab, mpair, mtwo, mpair_r, mtwo_r, tabv,
    tab_s, mtwo_s, tabx_s, tabr_s,
    lsem, msem, wsem, tsem, ssem1, rsem1, ssem2, rsem2, ssemy, rsemy,
):
    g = lax.axis_index("group")
    m = lax.axis_index("member")
    y, co = g // 2, g % 2
    z, x = m // 4, m % 4
    dev = g * MEM + m
    nxt = (dev + 1) % (GRP * MEM)
    prv = (dev + GRP * MEM - 1) % (GRP * MEM)

    loads = [
        *[
            pltpu.make_async_copy(fine_h.at[pl.ds(4 * i, 4)], fine.at[pl.ds(4 * i, 4)], lsem.at[5 + i])
            for i in range(4)
        ],
        pltpu.make_async_copy(ig_h, win.at[pl.ds(ROWS, ROWS)], lsem.at[0]),
        pltpu.make_async_copy(rhs_h, rhs, lsem.at[1]),
        pltpu.make_async_copy(pr1_h, pr1, lsem.at[2]),
        pltpu.make_async_copy(pr2_h, pr2, lsem.at[3]),
        pltpu.make_async_copy(dinv_h, dinv, lsem.at[4]),
    ]
    for cp in loads:
        cp.start()

    order = sorted(
        [(dz, dx) for dz in range(4) for dx in range(4)],
        key=lambda o: min(o[0], 4 - o[0]) + min(o[1], 4 - o[1]),
    )
    ahead = [((z + dz) % 4) * 4 + (x + dx) % 4 for dz, dx in order]
    behind = [((z + 4 - dz) % 4) * 4 + (x + 4 - dx) % 4 for dz, dx in order]
    mpeers = ahead[1:]
    gpeers = []
    for dy in (1, 3, 2, 0):
        for dc in range(2):
            if (dy, dc) != (0, 0):
                gpeers.append(((y + dy) % 4) * 2 + (co + dc) % 2)

    barrier = pltpu.get_barrier_semaphore()
    for t in mpeers:
        pl.semaphore_signal(barrier, inc=1, device_id=(g, t), device_id_type=MESH)
    for t in gpeers:
        pl.semaphore_signal(barrier, inc=1, device_id=(t, m), device_id_type=MESH)
    for t in (nxt, prv):
        pl.semaphore_signal(barrier, inc=1, device_id=(t // MEM, t % MEM), device_id_type=MESH)

    for e in range(ROWS):
        mpair[pl.ds(e, 1), :] = jnp.full((1, BLOCK), p1_s[e], I32)
    lane = lax.broadcasted_iota(I32, (1, BLOCK), 1)
    own2 = [p2_s[c] // (4 * MEM) for c in range(8)]
    for c in range(8):
        rank = jnp.int32(0)
        for b in range(c):
            rank = rank + jnp.where(own2[b] == own2[c], 1, 0)
        row = jnp.where(lane == 0, p2_s[c], jnp.minimum(rank, 1))
        for k in range(LINKS):
            row = jnp.where(lane == 1 + k, s2_s[c, k], row)
        mtwo[pl.ds(c, 1), :] = row
    for gp in range(GRP):
        a0 = jnp.int32(0)
        a1 = jnp.int32(0)
        for c in reversed(range(8)):
            hit = own2[c] == gp
            a1 = jnp.where(hit, a0, a1)
            a0 = jnp.where(hit, c, a0)
        tabx_s[2 * gp] = a0
        tabx_s[2 * gp + 1] = a1

    def slotted(s, first=0, count=ROWS):
        @pl.loop(first, first + count)
        def _(e):
            acc = jnp.where(s1_s[0, e] == s, 1.0, 0.0) * fine[e, 0]
            for k in range(1, LINKS):
                acc = acc + jnp.where(s1_s[k, e] == s, 1.0, 0.0) * fine[e, k]
            sb1[s, :, e] = acc.reshape(MEM, BAND, BLOCK)

    for i in range(4):
        loads[i].wait()
        slotted(0, 4 * i, 4)
    pl.semaphore_wait(barrier, MEM - 1 + GRP - 1 + 2)

    def remote(src, dst, ss, rs, dev_id):
        pltpu.make_async_remote_copy(
            src_ref=src, dst_ref=dst, send_sem=ss, recv_sem=rs, device_id=dev_id, device_id_type=MESH
        ).start()

    def local(src, dst, s):
        pltpu.make_async_copy(src, dst, s).start()

    def send1(s):
        for half in range(2):
            part = pl.ds(8 * half, 8)
            spot = pl.ds(pl.multiple_of(m * ROWS + 8 * half, 8), 8)
            for t in mpeers:
                remote(sb1.at[s, t, part], rb1[s].at[spot], ssem1.at[s], rsem1.at[s], (g, t))
        whole = pl.ds(pl.multiple_of(m * ROWS, ROWS), ROWS)
        local(sb1.at[s, m], rb1[s].at[whole], rsem1.at[s])

    def relay(s):
        def out(i):
            p, t = 4 * s + i // 4, ahead[i]
            src = srel.at[s, pl.ds(pl.multiple_of(t * 8, 8), 8)]
            if i == 0:
                local(src, rb2[p].at[0], rsem2.at[p])
            else:
                remote(src, rb2[p].at[i % 4], ssem2.at[s], rsem2.at[p], (g, t))

        for i in range(MEM):
            for b in range(8):
                c = ahead[i] * 8 + b
                srel[s, c] = rb1[s][tab_s[0, 0, c]] + rb1[s][tab_s[1, 0, c]]
            if i >= 1:
                out(i - 1)
        out(MEM - 1)

    def sendy(p):
        pltpu.make_async_copy(rb2[p], rb2[p], rsem2.at[p]).wait()
        for i, t in enumerate((*gpeers, g)):
            for j in range(2):
                sby[p, t, j] = rb2[p][:, tabx_s[2 * t + j]]
            if i >= 1:
                to = gpeers[i - 1]
                remote(sby.at[p, to], rby[p].at[g], ssemy.at[p // 4], rsemy.at[p], (to, m))
        local(sby.at[p, g], rby[p].at[g], rsemy.at[p])

    def addy(p):
        s = p // 4
        pltpu.make_async_copy(rby[p], rby[p], rsemy.at[p]).wait()

        @pl.loop(0, 4)
        def _(q):
            rs, ws = [], []
            for i in range(2):
                code = tabr_s[q * 2 + i]
                src = code // 8
                c = code % 8
                rs.append(rby[p][src, jnp.clip(mtwo_s[src, c, 6], 0, 1)])
                ws.append(mtwo_s[src, c, 1 + s])
            for t in range(LINKS):
                add = jnp.where(ws[0] == t, 1.0, 0.0) * rs[0] + jnp.where(ws[1] == t, 1.0, 0.0) * rs[1]
                for i in range(4):
                    b = behind[4 * (p % 4) + i]
                    if s == 0:
                        sum2[q * LINKS + t, b] = add[i]
                    else:
                        sum2[q * LINKS + t, b] = sum2[q * LINKS + t, b] + add[i]

    def wait1(s):
        pltpu.make_async_copy(rb1[s], rb1[s], rsem1.at[s]).wait()

    send1(0)
    for t in mpeers:
        remote(mpair, mpair_r.at[m], msem.at[0], msem.at[1], (g, t))
    local(mpair, mpair_r.at[m], msem.at[1])
    for t in gpeers:
        remote(mtwo, mtwo_r.at[g], msem.at[2], msem.at[3], (t, m))
    local(mtwo, mtwo_r.at[g], msem.at[3])

    slotted(1)
    send1(1)
    loads[4].wait()
    remote(
        win.at[pl.ds(ROWS, ROWS)], win.at[pl.ds(0, ROWS)], wsem.at[0], wsem.at[2],
        (nxt // MEM, nxt % MEM),
    )
    remote(
        win.at[pl.ds(ROWS, ROWS)], win.at[pl.ds(2 * ROWS, ROWS)], wsem.at[1], wsem.at[3],
        (prv // MEM, prv % MEM),
    )
    slotted(2)

    pltpu.make_async_copy(mpair_r, mpair_r, msem.at[1]).wait()
    cid = lax.broadcasted_iota(I32, (8, BLOCK), 1) + g * (MEM * 8)
    sub = lax.broadcasted_iota(I32, (8, BLOCK), 0)
    lo = jnp.full((8, BLOCK), 1 << 20, I32)
    hi = jnp.full((8, BLOCK), -1, I32)
    for src in range(MEM):
        for h in range(2):
            hit = mpair_r[src, pl.ds(8 * h, 8), :] == cid
            eid = sub + (src * ROWS + 8 * h)
            lo = jnp.minimum(lo, jnp.where(hit, eid, 1 << 20))
            hi = jnp.maximum(hi, jnp.where(hit, eid, -1))
    for sh in (4, 2, 1):
        lo = jnp.minimum(lo, pltpu.roll(lo, sh, 0))
        hi = jnp.maximum(hi, pltpu.roll(hi, sh, 0))
    tabv[0] = jnp.clip(lo, 0, MEM * ROWS - 1)
    tabv[1] = jnp.clip(hi, 0, MEM * ROWS - 1)
    pltpu.make_async_copy(mtwo_r, mtwo_r, msem.at[3]).wait()
    cp_t = pltpu.make_async_copy(tabv, tab_s, tsem.at[0])
    cp_t.start()
    cp_m = pltpu.make_async_copy(mtwo_r, mtwo_s, tsem.at[1])
    cp_m.start()
    cp_t.wait()
    cp_m.wait()
    qbase = dev * 4

    def scan(i, carry):
        v = mtwo_s[i // 8, i % 8, 0]
        out = []
        for q in range(4):
            p0, p1 = carry[2 * q], carry[2 * q + 1]
            hit = v == qbase + q
            out.append(jnp.where(hit, i, p0))
            out.append(jnp.where(hit, p0, p1))
        return tuple(out)

    found = lax.fori_loop(0, 64, scan, tuple(jnp.int32(0) for _ in range(8)))
    for i in range(8):
        tabr_s[i] = found[i]

    lanes = lax.broadcasted_iota(I32, (BLOCK, BLOCK), 1)
    total = GRP * MEM * ROWS

    def prod(e, cols):
        acc = jnp.zeros((BLOCK, BLOCK), F32)
        for k in range(LINKS):
            at = nb_s[k, e] - dev * ROWS + ROWS
            at = jnp.where(at < 0, at + total, jnp.where(at >= total, at - total, at))
            at = jnp.clip(at, 0, 3 * ROWS - 1)
            acc = acc + fine[e, k] * win[pl.ds(at, 1), :]
        return jnp.where(lanes == e, jnp.sum(acc, axis=1, keepdims=True), cols)

    def smooth(e, cols):
        acc = dinv[e] * rhs[pl.ds(e, 1), :]
        return jnp.where(lanes == e, jnp.sum(acc, axis=1, keepdims=True), cols)

    def sweep(part):
        if part == 0:
            for cp in loads[5:]:
                cp.wait()
            pltpu.make_async_copy(win.at[pl.ds(0, ROWS)], win.at[pl.ds(0, ROWS)], wsem.at[2]).wait()
            pltpu.make_async_copy(win.at[pl.ds(0, ROWS)], win.at[pl.ds(2 * ROWS, ROWS)], wsem.at[3]).wait()
            cols_v[...] = lax.fori_loop(0, 8, prod, jnp.zeros((BLOCK, BLOCK), F32))
        elif part == 1:
            cols = lax.fori_loop(8, ROWS, prod, cols_v[...])
            rhs[...] = rhs[...] - cols.T[:ROWS]
        else:
            cols = lax.fori_loop(0, ROWS, smooth, jnp.zeros((BLOCK, BLOCK), F32))
            smo_v[...] = win[pl.ds(ROWS, ROWS), :] + damping * cols.T[:ROWS]

    def products():
        p1 = pr1[...]
        qm = jnp.dot(p1, pr2[...], preferred_element_type=F32, precision=lax.Precision.HIGHEST)
        for i, a in enumerate((*spl(p1), *spl(p1.T))):
            ptab[i] = a
        for i, a in enumerate((*spl(qm), *spl(qm.T))):
            qtab[i] = a

    def coarse(s):
        for i in range(MEM):
            blk[:, behind[i]] = rb2[4 * s + i // 4][i % 4]

        @pl.loop(0, 2)
        def _(i):
            for b in range(4):
                c = i * 4 + b
                co1[c, s] = triple(blk[c].reshape(BLOCK, BLOCK), ptab)

    def hop(s, then):
        wait1(s)
        relay(s)
        if then is not None:
            send1(then)

    def up(s):
        for i in range(4):
            sendy(4 * s + i)
        coarse(s)

    def done(s):
        for i in range(4):
            addy(4 * s + i)

    hop(0, 2)
    sweep(0)
    slotted(3)
    products()
    hop(1, 3)
    slotted(4)
    up(0)
    sweep(1)
    hop(2, None)
    up(1)
    done(0)
    sweep(2)
    hop(3, 4)
    up(2)
    done(1)
    up(3)
    done(2)
    hop(4, None)
    up(4)
    done(3)
    done(4)
    for s in range(LINKS):
        pltpu.make_async_copy(sb1.at[s, pl.ds(0, MEM - 1)], sb1.at[s, pl.ds(0, MEM - 1)], ssem1.at[s]).wait()
        pltpu.make_async_copy(srel.at[s, pl.ds(0, 120)], srel.at[s, pl.ds(0, 120)], ssem2.at[s]).wait()
        pltpu.make_async_copy(
            sby.at[pl.ds(4 * s, 4), pl.ds(0, GRP - 1)], sby.at[pl.ds(4 * s, 4), pl.ds(0, GRP - 1)], ssemy.at[s]
        ).wait()
    pltpu.make_async_copy(mpair_r.at[pl.ds(0, MEM - 1)], mpair_r.at[pl.ds(0, MEM - 1)], msem.at[0]).wait()
    pltpu.make_async_copy(mtwo_r.at[pl.ds(0, GRP - 1)], mtwo_r.at[pl.ds(0, GRP - 1)], msem.at[2]).wait()
    for i in range(2):
        pltpu.make_async_copy(win.at[pl.ds(0, ROWS)], win.at[pl.ds(0, ROWS)], wsem.at[i]).wait()


def local(
    fine_blocks, neighbours, slot_one, pair_one, prolong_one, slot_two, pair_two, prolong_two,
    diag_inverse, right_side, initial_guess,
):
    smem = pl.BlockSpec(memory_space=pltpu.SMEM)
    hbm = pl.BlockSpec(memory_space=pltpu.HBM)
    vmem = pl.BlockSpec(memory_space=pltpu.VMEM)
    V, S, D = pltpu.VMEM, pltpu.SMEM, pltpu.SemaphoreType.DMA
    mid = pl.pallas_call(
        kernel,
        name="setup",
        out_shape=(
            V((8, LINKS, BLOCK, BLOCK), F32),
            V((4 * LINKS, MEM, BAND, BLOCK), F32),
            V((4, BLOCK, BLOCK), BF16),
            V((ROWS, BLOCK), F32),
        ),
        in_specs=[smem] * 5 + [hbm] * 6,
        out_specs=(vmem,) * 4,
        scratch_shapes=[
            V((ROWS, LINKS, BLOCK, BLOCK), F32),
            V((BLOCK, BLOCK), F32),
            V((BLOCK, BLOCK), F32),
            V((ROWS, BLOCK, BLOCK), F32),
            V((ROWS, BLOCK), F32),
            V((3 * ROWS, BLOCK), F32),
            V((LINKS, MEM, ROWS, BAND, BLOCK), F32),
            [V((MEM * ROWS, BAND, BLOCK), F32)] * LINKS,
            V((LINKS, MEM * 8, BAND, BLOCK), F32),
            [V((4, 8, BAND, BLOCK), F32)] * (4 * LINKS),
            V((4 * LINKS, GRP, 2, 4, BAND, BLOCK), F32),
            [V((GRP, 2, 4, BAND, BLOCK), F32)] * (4 * LINKS),
            V((8, MEM, BAND, BLOCK), F32),
            V((BLOCK, BLOCK), F32),
            V((4, BLOCK, BLOCK), BF16),
            V((ROWS, BLOCK), I32),
            V((8, BLOCK), I32),
            V((MEM, ROWS, BLOCK), I32),
            V((GRP, 8, BLOCK), I32),
            V((2, 8, BLOCK), I32),
            S((2, 8, BLOCK), I32),
            S((GRP, 8, BLOCK), I32),
            S((2 * GRP,), I32),
            S((8,), I32),
            D((9,)), D((4,)), D((4,)), D((2,)),
            D((LINKS,)), D((LINKS,)), D((LINKS,)), D((4 * LINKS,)), D((LINKS,)), D((4 * LINKS,)),
        ],
        compiler_params=pltpu.CompilerParams(
            collective_id=0, has_side_effects=True, vmem_limit_bytes=LIMIT
        ),
    )(
        neighbours.T, slot_one.T, pair_one, slot_two, pair_two,
        fine_blocks, prolong_one, prolong_two, diag_inverse, right_side, initial_guess,
    )
    co1, co2, smo = pl.pallas_call(
        finish,
        name="finish",
        out_shape=(
            jax.ShapeDtypeStruct((8, LINKS, BLOCK, BLOCK), F32),
            jax.ShapeDtypeStruct((4 * LINKS, BLOCK, BLOCK), F32),
            jax.ShapeDtypeStruct((ROWS, BLOCK), F32),
        ),
        in_specs=[vmem] * 4,
        out_specs=(hbm,) * 3,
        scratch_shapes=[V((4 * LINKS, BLOCK, BLOCK), F32), D((7,))],
        compiler_params=pltpu.CompilerParams(vmem_limit_bytes=16 * 1024 * 1024),
    )(*mid)
    return co1, co2.reshape(4, LINKS, BLOCK, BLOCK), smo


def solution(mesh):
    both = ("group", "member")
    return jax.shard_map(
        local,
        mesh=mesh,
        in_specs=(
            P(both, None, None, None), P(both, None), P(both, None), P(both), P(), P(both, None), P(both), P(),
            P(both, None, None), P(both, None), P(both, None),
        ),
        out_specs=(P(both, None, None, None), P(both, None, None, None), P(both, None)),
        check_vma=False,
    )
```

```python
import functools

import jax
import jax.numpy as jnp
from jax import lax
from jax.experimental import pallas as pl
from jax.experimental.pallas import tpu as pltpu
from jax.sharding import PartitionSpec as P

MESH = pl.DeviceIdType.MESH
F32 = jnp.float32
BF16 = jnp.bfloat16
I32 = jnp.int32
damping = 0.7

ROWS = 16
LINKS = 5
BLOCK = 128
MEM = 16
GRP = 8
BAND = BLOCK // MEM
LIMIT = 60 * 1024 * 1024


def spl(a):
    hi = a.astype(BF16)
    lo = (a - hi.astype(F32)).astype(BF16)
    return hi, lo


def dot3(a, b):
    d = functools.partial(jnp.dot, preferred_element_type=F32)
    return d(a[0], b[0]) + (d(a[0], b[1]) + d(a[1], b[0]))


def triple(blk, tab):
    right = dot3(spl(blk), (tab[0], tab[1]))
    return dot3((tab[2], tab[3]), spl(right))


def finish(co1, sum2, qtab, smo, co1_o, co2_o, smo_o, st2, sem):
    out = [
        pltpu.make_async_copy(co1, co1_o, sem.at[0]),
        pltpu.make_async_copy(smo, smo_o, sem.at[1]),
    ]
    for cp in out:
        cp.start()
    for i in range(5):
        for b in range(4):
            j = i * 4 + b
            st2[j] = triple(sum2[j].reshape(BLOCK, BLOCK), qtab)
        out.append(pltpu.make_async_copy(st2.at[pl.ds(4 * i, 4)], co2_o.at[pl.ds(4 * i, 4)], sem.at[2 + i]))
        out[-1].start()
    for cp in out:
        cp.wait()


def kernel(
    nb_h, s1_h, p1_h, s2_h, p2_h,
    fine_h, pr1_h, pr2_h, dinv_h, rhs_h, ig_h,
    co1, sum2, qtab, smo_v,
    fine, pr1, pr2, dinv, rhs, win,
    sb1, rb1, srel, rb2, sby, rby, blk, cols_v,
    ptab, mpair, mtwo, mpair_r, mtwo_r, tabv,
    nb_s, s1_s, p1_s, s2_s, p2_s, tab_s, mtwo_s, tabx_s, tabr_s,
    lsem, msem, wsem, tsem, ssem1, rsem1, ssem2, rsem2, ssemy, rsemy,
):
    g = lax.axis_index("group")
    m = lax.axis_index("member")
    y, co = g // 2, g % 2
    z, x = m // 4, m % 4
    dev = g * MEM + m
    nxt = (dev + 1) % (GRP * MEM)
    prv = (dev + GRP * MEM - 1) % (GRP * MEM)

    loads = [
        *[
            pltpu.make_async_copy(fine_h.at[pl.ds(4 * i, 4)], fine.at[pl.ds(4 * i, 4)], lsem.at[5 + i])
            for i in range(4)
        ],
        pltpu.make_async_copy(ig_h, win.at[pl.ds(ROWS, ROWS)], lsem.at[0]),
        pltpu.make_async_copy(rhs_h, rhs, lsem.at[1]),
        pltpu.make_async_copy(pr1_h, pr1, lsem.at[2]),
        pltpu.make_async_copy(pr2_h, pr2, lsem.at[3]),
        pltpu.make_async_copy(dinv_h, dinv, lsem.at[4]),
    ]
    ints = [
        pltpu.make_async_copy(a, b, tsem.at[2 + i])
        for i, (a, b) in enumerate(((s1_h, s1_s), (p1_h, p1_s), (p2_h, p2_s), (s2_h, s2_s), (nb_h, nb_s)))
    ]
    for cp in ints:
        cp.start()
    for cp in loads:
        cp.start()

    order = sorted(
        [(dz, dx) for dz in range(4) for dx in range(4)],
        key=lambda o: min(o[0], 4 - o[0]) + min(o[1], 4 - o[1]),
    )
    ahead = [((z + dz) % 4) * 4 + (x + dx) % 4 for dz, dx in order]
    behind = [((z + 4 - dz) % 4) * 4 + (x + 4 - dx) % 4 for dz, dx in order]
    mpeers = ahead[1:]
    gpeers = []
    for dy in (1, 3, 2, 0):
        for dc in range(2):
            if (dy, dc) != (0, 0):
                gpeers.append(((y + dy) % 4) * 2 + (co + dc) % 2)

    barrier = pltpu.get_barrier_semaphore()
    for t in mpeers:
        pl.semaphore_signal(barrier, inc=1, device_id=(g, t), device_id_type=MESH)
    for t in gpeers:
        pl.semaphore_signal(barrier, inc=1, device_id=(t, m), device_id_type=MESH)
    for t in (nxt, prv):
        pl.semaphore_signal(barrier, inc=1, device_id=(t // MEM, t % MEM), device_id_type=MESH)

    for cp in ints:
        cp.wait()
    for e in range(ROWS):
        mpair[pl.ds(e, 1), :] = jnp.full((1, BLOCK), p1_s[e], I32)
    lane = lax.broadcasted_iota(I32, (1, BLOCK), 1)
    own2 = [p2_s[c] // (4 * MEM) for c in range(8)]
    for c in range(8):
        rank = jnp.int32(0)
        for b in range(c):
            rank = rank + jnp.where(own2[b] == own2[c], 1, 0)
        row = jnp.where(lane == 0, p2_s[c], jnp.minimum(rank, 1))
        for k in range(LINKS):
            row = jnp.where(lane == 1 + k, s2_s[c, k], row)
        mtwo[pl.ds(c, 1), :] = row
    for gp in range(GRP):
        a0 = jnp.int32(0)
        a1 = jnp.int32(0)
        for c in reversed(range(8)):
            hit = own2[c] == gp
            a1 = jnp.where(hit, a0, a1)
            a0 = jnp.where(hit, c, a0)
        tabx_s[2 * gp] = a0
        tabx_s[2 * gp + 1] = a1

    def slotted(s, first=0, count=ROWS):
        @pl.loop(first, first + count)
        def _(e):
            acc = jnp.where(s1_s[0, e] == s, 1.0, 0.0) * fine[e, 0]
            for k in range(1, LINKS):
                acc = acc + jnp.where(s1_s[k, e] == s, 1.0, 0.0) * fine[e, k]
            sb1[s, :, e] = acc.reshape(MEM, BAND, BLOCK)

    for i in range(4):
        loads[i].wait()
        slotted(0, 4 * i, 4)
    pl.semaphore_wait(barrier, MEM - 1 + GRP - 1 + 2)

    def remote(src, dst, ss, rs, dev_id):
        pltpu.make_async_remote_copy(
            src_ref=src, dst_ref=dst, send_sem=ss, recv_sem=rs, device_id=dev_id, device_id_type=MESH
        ).start()

    def local(src, dst, s):
        pltpu.make_async_copy(src, dst, s).start()

    def send1(s, parts=range(4)):
        for part in parts:
            rows = pl.ds(4 * part, 4)
            spot = pl.ds(pl.multiple_of(m * ROWS + 4 * part, 4), 4)
            for t in mpeers:
                remote(sb1.at[s, t, rows], rb1[s].at[spot], ssem1.at[s], rsem1.at[s], (g, t))
            local(sb1.at[s, m, rows], rb1[s].at[spot], rsem1.at[s])

    def relay(s):
        def out(i):
            p, t = 4 * s + i // 4, ahead[i]
            src = srel.at[s, pl.ds(pl.multiple_of(t * 8, 8), 8)]
            if i == 0:
                local(src, rb2[p].at[0], rsem2.at[p])
            else:
                remote(src, rb2[p].at[i % 4], ssem2.at[s], rsem2.at[p], (g, t))

        for i in range(MEM):
            for b in range(8):
                c = ahead[i] * 8 + b
                srel[s, c] = rb1[s][tab_s[0, 0, c]] + rb1[s][tab_s[1, 0, c]]
            if i >= 1:
                out(i - 1)
        out(MEM - 1)

    def sendy(p):
        pltpu.make_async_copy(rb2[p], rb2[p], rsem2.at[p]).wait()
        for i, t in enumerate((*gpeers, g)):
            for j in range(2):
                sby[p, t, j] = rb2[p][:, tabx_s[2 * t + j]]
            if i >= 1:
                to = gpeers[i - 1]
                remote(sby.at[p, to], rby[p].at[g], ssemy.at[p // 4], rsemy.at[p], (to, m))
        local(sby.at[p, g], rby[p].at[g], rsemy.at[p])

    def addy(p):
        s = p // 4
        pltpu.make_async_copy(rby[p], rby[p], rsemy.at[p]).wait()

        @pl.loop(0, 4)
        def _(q):
            rs, ws = [], []
            for i in range(2):
                code = tabr_s[q * 2 + i]
                src = code // 8
                c = code % 8
                rs.append(rby[p][src, jnp.clip(mtwo_s[src, c, 6], 0, 1)])
                ws.append(mtwo_s[src, c, 1 + s])
            for t in range(LINKS):
                add = jnp.where(ws[0] == t, 1.0, 0.0) * rs[0] + jnp.where(ws[1] == t, 1.0, 0.0) * rs[1]
                for i in range(4):
                    b = behind[4 * (p % 4) + i]
                    if s == 0:
                        sum2[q * LINKS + t, b] = add[i]
                    else:
                        sum2[q * LINKS + t, b] = sum2[q * LINKS + t, b] + add[i]

    def wait1(s):
        pltpu.make_async_copy(rb1[s], rb1[s], rsem1.at[s]).wait()

    send1(0)
    for t in mpeers:
        remote(mpair, mpair_r.at[m], msem.at[0], msem.at[1], (g, t))
    local(mpair, mpair_r.at[m], msem.at[1])
    for t in gpeers:
        remote(mtwo, mtwo_r.at[g], msem.at[2], msem.at[3], (t, m))
    local(mtwo, mtwo_r.at[g], msem.at[3])

    slotted(1)
    send1(1)
    loads[4].wait()
    remote(
        win.at[pl.ds(ROWS, ROWS)], win.at[pl.ds(0, ROWS)], wsem.at[0], wsem.at[2],
        (nxt // MEM, nxt % MEM),
    )
    remote(
        win.at[pl.ds(ROWS, ROWS)], win.at[pl.ds(2 * ROWS, ROWS)], wsem.at[1], wsem.at[3],
        (prv // MEM, prv % MEM),
    )
    slotted(2)

    pltpu.make_async_copy(mpair_r, mpair_r, msem.at[1]).wait()
    cid = lax.broadcasted_iota(I32, (8, BLOCK), 1) + g * (MEM * 8)
    sub = lax.broadcasted_iota(I32, (8, BLOCK), 0)
    lo = jnp.full((8, BLOCK), 1 << 20, I32)
    hi = jnp.full((8, BLOCK), -1, I32)
    for src in range(MEM):
        for h in range(2):
            hit = mpair_r[src, pl.ds(8 * h, 8), :] == cid
            eid = sub + (src * ROWS + 8 * h)
            lo = jnp.minimum(lo, jnp.where(hit, eid, 1 << 20))
            hi = jnp.maximum(hi, jnp.where(hit, eid, -1))
    for sh in (4, 2, 1):
        lo = jnp.minimum(lo, pltpu.roll(lo, sh, 0))
        hi = jnp.maximum(hi, pltpu.roll(hi, sh, 0))
    tabv[0] = jnp.clip(lo, 0, MEM * ROWS - 1)
    tabv[1] = jnp.clip(hi, 0, MEM * ROWS - 1)
    pltpu.make_async_copy(mtwo_r, mtwo_r, msem.at[3]).wait()
    cp_t = pltpu.make_async_copy(tabv, tab_s, tsem.at[0])
    cp_t.start()
    cp_m = pltpu.make_async_copy(mtwo_r, mtwo_s, tsem.at[1])
    cp_m.start()
    cp_t.wait()
    cp_m.wait()
    qbase = dev * 4

    def scan(i, carry):
        v = mtwo_s[i // 8, i % 8, 0]
        out = []
        for q in range(4):
            p0, p1 = carry[2 * q], carry[2 * q + 1]
            hit = v == qbase + q
            out.append(jnp.where(hit, i, p0))
            out.append(jnp.where(hit, p0, p1))
        return tuple(out)

    found = lax.fori_loop(0, 64, scan, tuple(jnp.int32(0) for _ in range(8)))
    for i in range(8):
        tabr_s[i] = found[i]

    lanes = lax.broadcasted_iota(I32, (BLOCK, BLOCK), 1)
    total = GRP * MEM * ROWS

    def prod(e, cols):
        acc = jnp.zeros((BLOCK, BLOCK), F32)
        for k in range(LINKS):
            at = nb_s[k, e] - dev * ROWS + ROWS
            at = jnp.where(at < 0, at + total, jnp.where(at >= total, at - total, at))
            at = jnp.clip(at, 0, 3 * ROWS - 1)
            acc = acc + fine[e, k] * win[pl.ds(at, 1), :]
        return jnp.where(lanes == e, jnp.sum(acc, axis=1, keepdims=True), cols)

    def smooth(e, cols):
        acc = dinv[e] * rhs[pl.ds(e, 1), :]
        return jnp.where(lanes == e, jnp.sum(acc, axis=1, keepdims=True), cols)

    def sweep(part):
        if part == 0:
            for cp in loads[5:]:
                cp.wait()
            pltpu.make_async_copy(win.at[pl.ds(0, ROWS)], win.at[pl.ds(0, ROWS)], wsem.at[2]).wait()
            pltpu.make_async_copy(win.at[pl.ds(0, ROWS)], win.at[pl.ds(2 * ROWS, ROWS)], wsem.at[3]).wait()
            cols_v[...] = lax.fori_loop(0, 8, prod, jnp.zeros((BLOCK, BLOCK), F32))
        elif part == 1:
            cols = lax.fori_loop(8, ROWS, prod, cols_v[...])
            rhs[...] = rhs[...] - cols.T[:ROWS]
        else:
            cols = lax.fori_loop(0, ROWS, smooth, jnp.zeros((BLOCK, BLOCK), F32))
            smo_v[...] = win[pl.ds(ROWS, ROWS), :] + damping * cols.T[:ROWS]

    def products():
        p1 = pr1[...]
        qm = jnp.dot(p1, pr2[...], preferred_element_type=F32, precision=lax.Precision.HIGHEST)
        for i, a in enumerate((*spl(p1), *spl(p1.T))):
            ptab[i] = a
        for i, a in enumerate((*spl(qm), *spl(qm.T))):
            qtab[i] = a

    def coarse(s):
        for i in range(MEM):
            blk[:, behind[i]] = rb2[4 * s + i // 4][i % 4]

        @pl.loop(0, 2)
        def _(i):
            for b in range(4):
                c = i * 4 + b
                co1[c, s] = triple(blk[c].reshape(BLOCK, BLOCK), ptab)

    def hop(s, then):
        wait1(s)
        relay(s)
        if then is not None:
            send1(then)

    def up(s):
        for i in range(4):
            sendy(4 * s + i)
        coarse(s)

    def done(s):
        for i in range(4):
            addy(4 * s + i)

    hop(0, 2)
    sweep(0)
    slotted(3)
    products()
    hop(1, 3)
    slotted(4)
    up(0)
    sweep(1)
    hop(2, None)
    up(1)
    done(0)
    sweep(2)
    hop(3, 4)
    up(2)
    done(1)
    up(3)
    done(2)
    hop(4, None)
    for i in range(4):
        sendy(16 + i)
        addy(12 + i)
    coarse(4)
    done(4)
    for s in range(LINKS):
        pltpu.make_async_copy(sb1.at[s, pl.ds(0, MEM - 1)], sb1.at[s, pl.ds(0, MEM - 1)], ssem1.at[s]).wait()
        pltpu.make_async_copy(srel.at[s, pl.ds(0, 120)], srel.at[s, pl.ds(0, 120)], ssem2.at[s]).wait()
        pltpu.make_async_copy(
            sby.at[pl.ds(4 * s, 4), pl.ds(0, GRP - 1)], sby.at[pl.ds(4 * s, 4), pl.ds(0, GRP - 1)], ssemy.at[s]
        ).wait()
    pltpu.make_async_copy(mpair_r.at[pl.ds(0, MEM - 1)], mpair_r.at[pl.ds(0, MEM - 1)], msem.at[0]).wait()
    pltpu.make_async_copy(mtwo_r.at[pl.ds(0, GRP - 1)], mtwo_r.at[pl.ds(0, GRP - 1)], msem.at[2]).wait()
    for i in range(2):
        pltpu.make_async_copy(win.at[pl.ds(0, ROWS)], win.at[pl.ds(0, ROWS)], wsem.at[i]).wait()


def local(
    fine_blocks, neighbours, slot_one, pair_one, prolong_one, slot_two, pair_two, prolong_two,
    diag_inverse, right_side, initial_guess,
):
    hbm = pl.BlockSpec(memory_space=pltpu.HBM)
    vmem = pl.BlockSpec(memory_space=pltpu.VMEM)
    V, S, D = pltpu.VMEM, pltpu.SMEM, pltpu.SemaphoreType.DMA
    mid = pl.pallas_call(
        kernel,
        name="setup",
        out_shape=(
            V((8, LINKS, BLOCK, BLOCK), F32),
            V((4 * LINKS, MEM, BAND, BLOCK), F32),
            V((4, BLOCK, BLOCK), BF16),
            V((ROWS, BLOCK), F32),
        ),
        in_specs=[hbm] * 11,
        out_specs=(vmem,) * 4,
        scratch_shapes=[
            V((ROWS, LINKS, BLOCK, BLOCK), F32),
            V((BLOCK, BLOCK), F32),
            V((BLOCK, BLOCK), F32),
            V((ROWS, BLOCK, BLOCK), F32),
            V((ROWS, BLOCK), F32),
            V((3 * ROWS, BLOCK), F32),
            V((LINKS, MEM, ROWS, BAND, BLOCK), F32),
            [V((MEM * ROWS, BAND, BLOCK), F32)] * LINKS,
            V((LINKS, MEM * 8, BAND, BLOCK), F32),
            [V((4, 8, BAND, BLOCK), F32)] * (4 * LINKS),
            V((4 * LINKS, GRP, 2, 4, BAND, BLOCK), F32),
            [V((GRP, 2, 4, BAND, BLOCK), F32)] * (4 * LINKS),
            V((8, MEM, BAND, BLOCK), F32),
            V((BLOCK, BLOCK), F32),
            V((4, BLOCK, BLOCK), BF16),
            V((ROWS, BLOCK), I32),
            V((8, BLOCK), I32),
            V((MEM, ROWS, BLOCK), I32),
            V((GRP, 8, BLOCK), I32),
            V((2, 8, BLOCK), I32),
            S((LINKS, ROWS), I32), S((LINKS, ROWS), I32), S((ROWS,), I32), S((8, LINKS), I32), S((8,), I32),
            S((2, 8, BLOCK), I32),
            S((GRP, 8, BLOCK), I32),
            S((2 * GRP,), I32),
            S((8,), I32),
            D((9,)), D((4,)), D((4,)), D((7,)),
            D((LINKS,)), D((LINKS,)), D((LINKS,)), D((4 * LINKS,)), D((LINKS,)), D((4 * LINKS,)),
        ],
        compiler_params=pltpu.CompilerParams(
            collective_id=0, has_side_effects=True, vmem_limit_bytes=LIMIT
        ),
    )(
        neighbours.T, slot_one.T, pair_one, slot_two, pair_two,
        fine_blocks, prolong_one, prolong_two, diag_inverse, right_side, initial_guess,
    )
    co1, co2, smo = pl.pallas_call(
        finish,
        name="finish",
        out_shape=(
            jax.ShapeDtypeStruct((8, LINKS, BLOCK, BLOCK), F32),
            jax.ShapeDtypeStruct((4 * LINKS, BLOCK, BLOCK), F32),
            jax.ShapeDtypeStruct((ROWS, BLOCK), F32),
        ),
        in_specs=[vmem] * 4,
        out_specs=(hbm,) * 3,
        scratch_shapes=[V((4 * LINKS, BLOCK, BLOCK), F32), D((7,))],
        compiler_params=pltpu.CompilerParams(vmem_limit_bytes=16 * 1024 * 1024),
    )(*mid)
    return co1, co2.reshape(4, LINKS, BLOCK, BLOCK), smo


def solution(mesh):
    both = ("group", "member")
    return jax.shard_map(
        local,
        mesh=mesh,
        in_specs=(
            P(both, None, None, None), P(both, None), P(both, None), P(both), P(), P(both, None), P(both), P(),
            P(both, None, None), P(both, None), P(both, None),
        ),
        out_specs=(P(both, None, None, None), P(both, None, None, None), P(both, None)),
        check_vma=False,
    )
```

```python
import functools

import jax
import jax.numpy as jnp
from jax import lax
from jax.experimental import pallas as pl
from jax.experimental.pallas import tpu as pltpu
from jax.sharding import PartitionSpec as P

MESH = pl.DeviceIdType.MESH
F32 = jnp.float32
BF16 = jnp.bfloat16
I32 = jnp.int32
damping = 0.7

ROWS = 16
LINKS = 5
BLOCK = 128
MEM = 16
GRP = 8
BAND = BLOCK // MEM
LIMIT = 60 * 1024 * 1024


def spl(a):
    hi = a.astype(BF16)
    lo = (a - hi.astype(F32)).astype(BF16)
    return hi, lo


def dot3(a, b):
    d = functools.partial(jnp.dot, preferred_element_type=F32)
    return d(a[0], b[0]) + (d(a[0], b[1]) + d(a[1], b[0]))


def triple(blk, tab):
    right = dot3(spl(blk), (tab[0], tab[1]))
    return dot3((tab[2], tab[3]), spl(right))


def finish(co1, sum2, qtab, smo, co1_o, co2_o, smo_o, st2, sem):
    out = [
        pltpu.make_async_copy(co1, co1_o, sem.at[0]),
        pltpu.make_async_copy(smo, smo_o, sem.at[1]),
    ]
    for cp in out:
        cp.start()
    for i in range(5):
        for b in range(4):
            j = i * 4 + b
            st2[j] = triple(sum2[j].reshape(BLOCK, BLOCK), qtab)
        out.append(pltpu.make_async_copy(st2.at[pl.ds(4 * i, 4)], co2_o.at[pl.ds(4 * i, 4)], sem.at[2 + i]))
        out[-1].start()
    for cp in out:
        cp.wait()


def kernel(
    nb_h, s1_h, p1_h, s2_h, p2_h,
    fine_h, pr1_h, pr2_h, dinv_h, rhs_h, ig_h,
    co1, sum2, qtab, smo_v,
    fine, pr1, pr2, dinv, rhs, win,
    sb1, rb1, srel, rb2, sby, rby, blk, cols_v,
    ptab, mpair, mtwo, mpair_r, mtwo_r, tabv,
    nb_s, s1_s, p1_s, s2_s, p2_s, tab_s, mtwo_s, tabx_s, tabr_s,
    lsem, msem, wsem, tsem, ssem1, rsem1, ssem2, rsem2, ssemy, rsemy,
):
    g = lax.axis_index("group")
    m = lax.axis_index("member")
    y, co = g // 2, g % 2
    z, x = m // 4, m % 4
    dev = g * MEM + m
    nxt = (dev + 1) % (GRP * MEM)
    prv = (dev + GRP * MEM - 1) % (GRP * MEM)

    loads = [
        *[
            pltpu.make_async_copy(fine_h.at[pl.ds(4 * i, 4)], fine.at[pl.ds(4 * i, 4)], lsem.at[5 + i])
            for i in range(4)
        ],
        pltpu.make_async_copy(ig_h, win.at[pl.ds(ROWS, ROWS)], lsem.at[0]),
        pltpu.make_async_copy(rhs_h, rhs, lsem.at[1]),
        pltpu.make_async_copy(pr1_h, pr1, lsem.at[2]),
        pltpu.make_async_copy(pr2_h, pr2, lsem.at[3]),
        pltpu.make_async_copy(dinv_h, dinv, lsem.at[4]),
    ]
    ints = [
        pltpu.make_async_copy(a, b, tsem.at[2 + i])
        for i, (a, b) in enumerate(((s1_h, s1_s), (p1_h, p1_s), (p2_h, p2_s), (s2_h, s2_s), (nb_h, nb_s)))
    ]
    for cp in ints:
        cp.start()
    for cp in loads:
        cp.start()

    order = sorted(
        [(dz, dx) for dz in range(4) for dx in range(4)],
        key=lambda o: min(o[0], 4 - o[0]) + min(o[1], 4 - o[1]),
    )
    ahead = [((z + dz) % 4) * 4 + (x + dx) % 4 for dz, dx in order]
    behind = [((z + 4 - dz) % 4) * 4 + (x + 4 - dx) % 4 for dz, dx in order]
    mpeers = ahead[1:]
    gpeers = []
    for dy in (1, 3, 2, 0):
        for dc in range(2):
            if (dy, dc) != (0, 0):
                gpeers.append(((y + dy) % 4) * 2 + (co + dc) % 2)

    barrier = pltpu.get_barrier_semaphore()
    for t in mpeers:
        pl.semaphore_signal(barrier, inc=1, device_id=(g, t), device_id_type=MESH)
    for t in gpeers:
        pl.semaphore_signal(barrier, inc=1, device_id=(t, m), device_id_type=MESH)
    for t in (nxt, prv):
        pl.semaphore_signal(barrier, inc=1, device_id=(t // MEM, t % MEM), device_id_type=MESH)

    for cp in ints:
        cp.wait()
    for e in range(ROWS):
        mpair[pl.ds(e, 1), :] = jnp.full((1, BLOCK), p1_s[e], I32)
    lane = lax.broadcasted_iota(I32, (1, BLOCK), 1)
    own2 = [p2_s[c] // (4 * MEM) for c in range(8)]
    for c in range(8):
        rank = jnp.int32(0)
        for b in range(c):
            rank = rank + jnp.where(own2[b] == own2[c], 1, 0)
        row = jnp.where(lane == 0, p2_s[c], jnp.minimum(rank, 1))
        for k in range(LINKS):
            row = jnp.where(lane == 1 + k, s2_s[c, k], row)
        mtwo[pl.ds(c, 1), :] = row
    for gp in range(GRP):
        a0 = jnp.int32(0)
        a1 = jnp.int32(0)
        for c in reversed(range(8)):
            hit = own2[c] == gp
            a1 = jnp.where(hit, a0, a1)
            a0 = jnp.where(hit, c, a0)
        tabx_s[2 * gp] = a0
        tabx_s[2 * gp + 1] = a1

    def slotted(s, first=0, count=ROWS):
        @pl.loop(first, first + count)
        def _(e):
            acc = jnp.where(s1_s[0, e] == s, 1.0, 0.0) * fine[e, 0]
            for k in range(1, LINKS):
                acc = acc + jnp.where(s1_s[k, e] == s, 1.0, 0.0) * fine[e, k]
            sb1[s, :, e] = acc.reshape(MEM, BAND, BLOCK)

    for i in range(4):
        loads[i].wait()
        slotted(0, 4 * i, 4)
    pl.semaphore_wait(barrier, MEM - 1 + GRP - 1 + 2)

    def remote(src, dst, ss, rs, dev_id):
        pltpu.make_async_remote_copy(
            src_ref=src, dst_ref=dst, send_sem=ss, recv_sem=rs, device_id=dev_id, device_id_type=MESH
        ).start()

    def local(src, dst, s):
        pltpu.make_async_copy(src, dst, s).start()

    def send1(s, parts=range(4)):
        for part in parts:
            rows = pl.ds(4 * part, 4)
            spot = pl.ds(pl.multiple_of(m * ROWS + 4 * part, 4), 4)
            for t in mpeers:
                remote(sb1.at[s, t, rows], rb1[s].at[spot], ssem1.at[s], rsem1.at[s], (g, t))
            local(sb1.at[s, m, rows], rb1[s].at[spot], rsem1.at[s])

    def relay(s):
        def out(i):
            p, t = 4 * s + i // 4, ahead[i]
            src = srel.at[s, pl.ds(pl.multiple_of(t * 8, 8), 8)]
            if i == 0:
                local(src, rb2[p].at[0], rsem2.at[p])
            else:
                remote(src, rb2[p].at[i % 4], ssem2.at[s], rsem2.at[p], (g, t))

        for i in range(MEM):
            for b in range(8):
                c = ahead[i] * 8 + b
                srel[s, c] = rb1[s][tab_s[0, 0, c]] + rb1[s][tab_s[1, 0, c]]
            if i >= 1:
                out(i - 1)
        out(MEM - 1)

    def sendy(p):
        pltpu.make_async_copy(rb2[p], rb2[p], rsem2.at[p]).wait()
        for i, t in enumerate((*gpeers, g)):
            for j in range(2):
                sby[p, t, j] = rb2[p][:, tabx_s[2 * t + j]]
            if i >= 1:
                to = gpeers[i - 1]
                remote(sby.at[p, to], rby[p].at[g], ssemy.at[p // 4], rsemy.at[p], (to, m))
        local(sby.at[p, g], rby[p].at[g], rsemy.at[p])

    def addy(p):
        s = p // 4
        pltpu.make_async_copy(rby[p], rby[p], rsemy.at[p]).wait()

        @pl.loop(0, 4)
        def _(q):
            rs, ws = [], []
            for i in range(2):
                code = tabr_s[q * 2 + i]
                src = code // 8
                c = code % 8
                rs.append(rby[p][src, jnp.clip(mtwo_s[src, c, 6], 0, 1)])
                ws.append(mtwo_s[src, c, 1 + s])
            for t in range(LINKS):
                add = jnp.where(ws[0] == t, 1.0, 0.0) * rs[0] + jnp.where(ws[1] == t, 1.0, 0.0) * rs[1]
                for i in range(4):
                    b = behind[4 * (p % 4) + i]
                    if s == 0:
                        sum2[q * LINKS + t, b] = add[i]
                    else:
                        sum2[q * LINKS + t, b] = sum2[q * LINKS + t, b] + add[i]

    def wait1(s):
        pltpu.make_async_copy(rb1[s], rb1[s], rsem1.at[s]).wait()

    send1(0)
    for t in mpeers:
        remote(mpair, mpair_r.at[m], msem.at[0], msem.at[1], (g, t))
    local(mpair, mpair_r.at[m], msem.at[1])
    for t in gpeers:
        remote(mtwo, mtwo_r.at[g], msem.at[2], msem.at[3], (t, m))
    local(mtwo, mtwo_r.at[g], msem.at[3])

    slotted(1)
    send1(1)
    loads[4].wait()
    remote(
        win.at[pl.ds(ROWS, ROWS)], win.at[pl.ds(0, ROWS)], wsem.at[0], wsem.at[2],
        (nxt // MEM, nxt % MEM),
    )
    remote(
        win.at[pl.ds(ROWS, ROWS)], win.at[pl.ds(2 * ROWS, ROWS)], wsem.at[1], wsem.at[3],
        (prv // MEM, prv % MEM),
    )
    slotted(2)
    send1(2, (0,))
    slotted(3)

    pltpu.make_async_copy(mpair_r, mpair_r, msem.at[1]).wait()
    cid = lax.broadcasted_iota(I32, (8, BLOCK), 1) + g * (MEM * 8)
    sub = lax.broadcasted_iota(I32, (8, BLOCK), 0)
    lo = jnp.full((8, BLOCK), 1 << 20, I32)
    hi = jnp.full((8, BLOCK), -1, I32)
    for src in range(MEM):
        for h in range(2):
            hit = mpair_r[src, pl.ds(8 * h, 8), :] == cid
            eid = sub + (src * ROWS + 8 * h)
            lo = jnp.minimum(lo, jnp.where(hit, eid, 1 << 20))
            hi = jnp.maximum(hi, jnp.where(hit, eid, -1))
    for sh in (4, 2, 1):
        lo = jnp.minimum(lo, pltpu.roll(lo, sh, 0))
        hi = jnp.maximum(hi, pltpu.roll(hi, sh, 0))
    tabv[0] = jnp.clip(lo, 0, MEM * ROWS - 1)
    tabv[1] = jnp.clip(hi, 0, MEM * ROWS - 1)
    pltpu.make_async_copy(mtwo_r, mtwo_r, msem.at[3]).wait()
    cp_t = pltpu.make_async_copy(tabv, tab_s, tsem.at[0])
    cp_t.start()
    cp_m = pltpu.make_async_copy(mtwo_r, mtwo_s, tsem.at[1])
    cp_m.start()
    cp_t.wait()
    cp_m.wait()
    qbase = dev * 4

    def scan(i, carry):
        v = mtwo_s[i // 8, i % 8, 0]
        out = []
        for q in range(4):
            p0, p1 = carry[2 * q], carry[2 * q + 1]
            hit = v == qbase + q
            out.append(jnp.where(hit, i, p0))
            out.append(jnp.where(hit, p0, p1))
        return tuple(out)

    found = lax.fori_loop(0, 64, scan, tuple(jnp.int32(0) for _ in range(8)))
    for i in range(8):
        tabr_s[i] = found[i]

    lanes = lax.broadcasted_iota(I32, (BLOCK, BLOCK), 1)
    total = GRP * MEM * ROWS

    def prod(e, cols):
        acc = jnp.zeros((BLOCK, BLOCK), F32)
        for k in range(LINKS):
            at = nb_s[k, e] - dev * ROWS + ROWS
            at = jnp.where(at < 0, at + total, jnp.where(at >= total, at - total, at))
            at = jnp.clip(at, 0, 3 * ROWS - 1)
            acc = acc + fine[e, k] * win[pl.ds(at, 1), :]
        return jnp.where(lanes == e, jnp.sum(acc, axis=1, keepdims=True), cols)

    def smooth(e, cols):
        acc = dinv[e] * rhs[pl.ds(e, 1), :]
        return jnp.where(lanes == e, jnp.sum(acc, axis=1, keepdims=True), cols)

    def sweep(part):
        if part == 0:
            for cp in loads[5:]:
                cp.wait()
            pltpu.make_async_copy(win.at[pl.ds(0, ROWS)], win.at[pl.ds(0, ROWS)], wsem.at[2]).wait()
            pltpu.make_async_copy(win.at[pl.ds(0, ROWS)], win.at[pl.ds(2 * ROWS, ROWS)], wsem.at[3]).wait()
            cols_v[...] = lax.fori_loop(0, 8, prod, jnp.zeros((BLOCK, BLOCK), F32))
        elif part == 1:
            cols = lax.fori_loop(8, ROWS, prod, cols_v[...])
            rhs[...] = rhs[...] - cols.T[:ROWS]
        else:
            cols = lax.fori_loop(0, ROWS, smooth, jnp.zeros((BLOCK, BLOCK), F32))
            smo_v[...] = win[pl.ds(ROWS, ROWS), :] + damping * cols.T[:ROWS]

    def products():
        p1 = pr1[...]
        qm = jnp.dot(p1, pr2[...], preferred_element_type=F32, precision=lax.Precision.HIGHEST)
        for i, a in enumerate((*spl(p1), *spl(p1.T))):
            ptab[i] = a
        for i, a in enumerate((*spl(qm), *spl(qm.T))):
            qtab[i] = a

    def coarse(s):
        for i in range(MEM):
            blk[:, behind[i]] = rb2[4 * s + i // 4][i % 4]

        @pl.loop(0, 2)
        def _(i):
            for b in range(4):
                c = i * 4 + b
                co1[c, s] = triple(blk[c].reshape(BLOCK, BLOCK), ptab)

    def hop(s, *then):
        wait1(s)
        relay(s)
        for t in then:
            send1(*t)

    def up(s):
        for i in range(4):
            sendy(4 * s + i)
        coarse(s)

    def done(s):
        for i in range(4):
            addy(4 * s + i)

    hop(0, (2, (1, 2, 3)), (3, (0,)))
    sweep(0)
    products()
    hop(1, (3, (1, 2, 3)))
    slotted(4)
    up(0)
    sweep(1)
    hop(2, (4, (0,)))
    up(1)
    done(0)
    sweep(2)
    hop(3, (4, (1, 2, 3)))
    up(2)
    done(1)
    up(3)
    done(2)
    hop(4)
    for i in range(4):
        sendy(16 + i)
        addy(12 + i)
    coarse(4)
    done(4)
    for s in range(LINKS):
        pltpu.make_async_copy(sb1.at[s, pl.ds(0, MEM - 1)], sb1.at[s, pl.ds(0, MEM - 1)], ssem1.at[s]).wait()
        pltpu.make_async_copy(srel.at[s, pl.ds(0, 120)], srel.at[s, pl.ds(0, 120)], ssem2.at[s]).wait()
        pltpu.make_async_copy(
            sby.at[pl.ds(4 * s, 4), pl.ds(0, GRP - 1)], sby.at[pl.ds(4 * s, 4), pl.ds(0, GRP - 1)], ssemy.at[s]
        ).wait()
    pltpu.make_async_copy(mpair_r.at[pl.ds(0, MEM - 1)], mpair_r.at[pl.ds(0, MEM - 1)], msem.at[0]).wait()
    pltpu.make_async_copy(mtwo_r.at[pl.ds(0, GRP - 1)], mtwo_r.at[pl.ds(0, GRP - 1)], msem.at[2]).wait()
    for i in range(2):
        pltpu.make_async_copy(win.at[pl.ds(0, ROWS)], win.at[pl.ds(0, ROWS)], wsem.at[i]).wait()


def local(
    fine_blocks, neighbours, slot_one, pair_one, prolong_one, slot_two, pair_two, prolong_two,
    diag_inverse, right_side, initial_guess,
):
    hbm = pl.BlockSpec(memory_space=pltpu.HBM)
    vmem = pl.BlockSpec(memory_space=pltpu.VMEM)
    V, S, D = pltpu.VMEM, pltpu.SMEM, pltpu.SemaphoreType.DMA
    mid = pl.pallas_call(
        kernel,
        name="setup",
        out_shape=(
            V((8, LINKS, BLOCK, BLOCK), F32),
            V((4 * LINKS, MEM, BAND, BLOCK), F32),
            V((4, BLOCK, BLOCK), BF16),
            V((ROWS, BLOCK), F32),
        ),
        in_specs=[hbm] * 11,
        out_specs=(vmem,) * 4,
        scratch_shapes=[
            V((ROWS, LINKS, BLOCK, BLOCK), F32),
            V((BLOCK, BLOCK), F32),
            V((BLOCK, BLOCK), F32),
            V((ROWS, BLOCK, BLOCK), F32),
            V((ROWS, BLOCK), F32),
            V((3 * ROWS, BLOCK), F32),
            V((LINKS, MEM, ROWS, BAND, BLOCK), F32),
            [V((MEM * ROWS, BAND, BLOCK), F32)] * LINKS,
            V((LINKS, MEM * 8, BAND, BLOCK), F32),
            [V((4, 8, BAND, BLOCK), F32)] * (4 * LINKS),
            V((4 * LINKS, GRP, 2, 4, BAND, BLOCK), F32),
            [V((GRP, 2, 4, BAND, BLOCK), F32)] * (4 * LINKS),
            V((8, MEM, BAND, BLOCK), F32),
            V((BLOCK, BLOCK), F32),
            V((4, BLOCK, BLOCK), BF16),
            V((ROWS, BLOCK), I32),
            V((8, BLOCK), I32),
            V((MEM, ROWS, BLOCK), I32),
            V((GRP, 8, BLOCK), I32),
            V((2, 8, BLOCK), I32),
            S((LINKS, ROWS), I32), S((LINKS, ROWS), I32), S((ROWS,), I32), S((8, LINKS), I32), S((8,), I32),
            S((2, 8, BLOCK), I32),
            S((GRP, 8, BLOCK), I32),
            S((2 * GRP,), I32),
            S((8,), I32),
            D((9,)), D((4,)), D((4,)), D((7,)),
            D((LINKS,)), D((LINKS,)), D((LINKS,)), D((4 * LINKS,)), D((LINKS,)), D((4 * LINKS,)),
        ],
        compiler_params=pltpu.CompilerParams(
            collective_id=0, has_side_effects=True, vmem_limit_bytes=LIMIT
        ),
    )(
        neighbours.T, slot_one.T, pair_one, slot_two, pair_two,
        fine_blocks, prolong_one, prolong_two, diag_inverse, right_side, initial_guess,
    )
    co1, co2, smo = pl.pallas_call(
        finish,
        name="finish",
        out_shape=(
            jax.ShapeDtypeStruct((8, LINKS, BLOCK, BLOCK), F32),
            jax.ShapeDtypeStruct((4 * LINKS, BLOCK, BLOCK), F32),
            jax.ShapeDtypeStruct((ROWS, BLOCK), F32),
        ),
        in_specs=[vmem] * 4,
        out_specs=(hbm,) * 3,
        scratch_shapes=[V((4 * LINKS, BLOCK, BLOCK), F32), D((7,))],
        compiler_params=pltpu.CompilerParams(vmem_limit_bytes=16 * 1024 * 1024),
    )(*mid)
    return co1, co2.reshape(4, LINKS, BLOCK, BLOCK), smo


def solution(mesh):
    both = ("group", "member")
    return jax.shard_map(
        local,
        mesh=mesh,
        in_specs=(
            P(both, None, None, None), P(both, None), P(both, None), P(both), P(), P(both, None), P(both), P(),
            P(both, None, None), P(both, None), P(both, None),
        ),
        out_specs=(P(both, None, None, None), P(both, None, None, None), P(both, None)),
        check_vma=False,
    )
```
